128 devices in a mesh: lon: 64 (over z_hi, x, y, core), lat: 2 (over z_lo).
Axes of the slice: x: 4, y: 4, z: 4 (z_hi: 2, z_lo: 2; z = z_hi * 2 + z_lo), core: 2. Of those that a mesh axis runs over, the one named last changes fastest.
Arguments:
- fields: float32 [128, 256, 4, 768], P('lat', 'lon'), may hold values from -24 to 24
- norm_gains: float32 [4, 768], replicated, may hold values from 0.25 to 1.75
- qkv_weight: bfloat16 [3, 768, 2304], replicated, may hold values from -0.21875 to 0.21875
- out_weight: bfloat16 [3, 768, 768], replicated, may hold values from -0.21875 to 0.21875
- longitude_bias: float32 [12, 256], replicated, may hold values from -3 to 380
- latitude_bias: float32 [12, 255], replicated, may hold values from -3 to 380
- level_bias: float32 [12, 7], replicated, may hold values from -3 to 380
- mlp_in: bfloat16 [768, 3072], replicated, may hold values from -0.21875 to 0.21875
- mlp_out: bfloat16 [3072, 768], replicated, may hold values from -0.109375 to 0.109375
Outputs:
- block_out: float32 [128, 256, 4, 768], P('lat', 'lon')
The draws below stay inside these ranges and needn't reach their ends.
All inputs are finite; a program needn't handle non-finite values.
Results may differ from the reference program's by a relative error of at most 0.013.
Values may be sent and summed in bfloat16 or wider, within the bound.
No kernel may reach another device: no remote copies, remote signals or barrier semaphores. Data moves between devices by JAX's collectives and lax.ppermute only.
A program may use at most 192 MiB of HBM per device.

```python
import jax
import jax.numpy as jnp
from jax import lax

D = 768
HEADS = 12
FF = 3072
LEV = 4
NLAT = 128
NLON = 256


def draw_fields(key, part):
    full_shape = (NLAT, NLON, LEV, D)
    key_base, key_rows, key_channels = jax.random.split(key, 3)
    random_part = jax.random.normal(key_base, full_shape, jnp.float32)
    row_scale = jnp.exp(jax.random.uniform(key_rows, (NLAT, NLON, LEV, 1), jnp.float32, jnp.log(0.3), jnp.log(3.0)))
    channels = jnp.exp(jax.random.uniform(key_channels, (D,), jnp.float32, jnp.log(0.3), jnp.log(3.0)))
    values = random_part * row_scale * channels
    return jnp.clip(values, -24.0, 24.0)


def plant(key, length):
    key_base = jax.random.fold_in(key, 0)
    lookup = jax.random.uniform(key_base, (HEADS, length), jnp.float32, -3.0, 3.0)
    return lookup


def draw_longitude_bias(key, part):
    return plant(jax.random.fold_in(key, 11), NLON)


def draw_latitude_bias(key, part):
    return plant(jax.random.fold_in(key, 12), 2 * NLAT - 1)


def draw_level_bias(key, part):
    return plant(jax.random.fold_in(key, 13), 2 * LEV - 1)


def scatter_about(stream_key, dims, spread, limit, kind=jnp.bfloat16):
    result = jax.random.normal(stream_key, dims, jnp.float32) * spread
    return jnp.minimum(jnp.maximum(result, -limit), limit).astype(kind)


def setup_inputs(seed: int = 0) -> dict:
    splits = jax.random.split(jax.random.key(seed), 10)
    return {
        "fields": draw_fields(jax.random.fold_in(splits[9], 71), 0),
        "norm_gains": jnp.clip(1.0 + 0.15 * jax.random.normal(splits[1], (4, D), jnp.float32), 0.25, 1.75),
        "qkv_weight": scatter_about(splits[2], (3, D, 3 * D), D ** -0.5, 0.21875),
        "out_weight": scatter_about(splits[3], (3, D, D), D ** -0.5, 0.21875),
        "longitude_bias": draw_longitude_bias(jax.random.fold_in(splits[9], 71), 0),
        "latitude_bias": draw_latitude_bias(jax.random.fold_in(splits[9], 71), 0),
        "level_bias": draw_level_bias(jax.random.fold_in(splits[9], 71), 0),
        "mlp_in": scatter_about(splits[7], (D, FF), D ** -0.5, 0.21875),
        "mlp_out": scatter_about(splits[8], (FF, D), FF ** -0.5, 0.109375),
    }


epsilon = 1e-06
group_rows = 8

def normalize(fields, gain_row):
    square = lax.optimization_barrier(jnp.mean(fields * fields, axis=-1, keepdims=True))
    return (fields * lax.rsqrt(square + epsilon) * gain_row).astype(jnp.bfloat16)

def project(fields, gain_row, weight):
    features = fields.shape[-1]
    normed = normalize(fields, gain_row).reshape(-1, features)
    projected = jnp.dot(normed, weight, preferred_element_type=jnp.float32).astype(jnp.bfloat16)
    head_shape = fields.shape[:-1] + (HEADS, features // HEADS)
    return tuple((projected[:, member * features:(member + 1) * features].reshape(head_shape) for member in range(3)))

def attend(queries, key_rows, values, position_bias, position):
    letters = ['a', 'b', 'c']
    query_form = ''.join(('i' if member == position else letters[member] for member in range(3)))
    key_form = ''.join(('j' if member == position else letters[member] for member in range(3)))
    batch_form = ''.join((letters[member] for member in range(3) if member != position))
    inverse_root = queries.shape[-1] ** (-0.5)
    scores = jnp.einsum(query_form + 'he,' + key_form + 'he->' + batch_form + 'hij', queries.astype(jnp.float32), key_rows.astype(jnp.float32))
    weights = jax.nn.softmax(scores * inverse_root + position_bias, axis=-1).astype(jnp.bfloat16)
    attended = jnp.einsum(batch_form + 'hij,' + key_form + 'he->' + query_form + 'he', weights.astype(jnp.float32), values.astype(jnp.float32))
    return attended.astype(jnp.bfloat16)

def finish(fields, attended, out_rows):
    features = fields.shape[-1]
    update = jnp.dot(attended.reshape(-1, features), out_rows, preferred_element_type=jnp.float32)
    return fields + update.reshape(fields.shape)

def sweep(fields, position, gain_row, qkv_rows, out_rows, position_bias):
    queries, key_rows, values = project(fields, gain_row, qkv_rows)
    return finish(fields, attend(queries, key_rows, values, position_bias, position), out_rows)

def feed_forward(fields, gain_row, weight_in, weight_out):
    features = fields.shape[-1]
    normed = normalize(fields, gain_row).reshape(-1, features)
    hidden = jax.nn.gelu(jnp.dot(normed, weight_in, preferred_element_type=jnp.float32), approximate=True).astype(jnp.bfloat16)
    return fields + jnp.dot(hidden, weight_out, preferred_element_type=jnp.float32).reshape(fields.shape)

def toeplitz(window, row_count, col_count):
    heads = window.shape[0]
    width = row_count + col_count - 1
    padded = jnp.concatenate([window, jnp.zeros((heads, 1), window.dtype)], axis=1)
    flat = jnp.tile(padded, (1, row_count))[:, :row_count * width]
    return flat.reshape(heads, row_count, width)[:, :, row_count - 1:]

def periodic_bias(lookup):
    length = lookup.shape[1]
    window = jnp.concatenate([lookup[:, 1:], lookup], axis=1)
    return toeplitz(window, length, length)

def open_bias(lookup, first_row, query_count):
    length = (lookup.shape[1] + 1) // 2
    start = length - query_count - first_row
    window = lax.dynamic_slice_in_dim(lookup, start, query_count + length - 1, 1)
    return toeplitz(window, query_count, length)

def in_groups(function, fields, mapped_axis):
    leading = jnp.moveaxis(fields, mapped_axis, 0)
    groups = leading.reshape((leading.shape[0] // group_rows, group_rows) + leading.shape[1:])
    outputs = lax.map(lambda pencils: jnp.moveaxis(function(jnp.moveaxis(pencils, 0, mapped_axis)), mapped_axis, 0), groups)
    return jnp.moveaxis(outputs.reshape(leading.shape), 0, mapped_axis)

def reference(fields, norm_gains, qkv_weight, out_weight, longitude_bias, latitude_bias, level_bias, mlp_in, mlp_out):
    beside_all = periodic_bias(longitude_bias)
    meridian = open_bias(latitude_bias, 0, NLAT)
    column = open_bias(level_bias, 0, LEV)
    state = in_groups(lambda pencils: sweep(pencils, 1, norm_gains[0], qkv_weight[0], out_weight[0], beside_all), fields, 0)
    state = in_groups(lambda pencils: sweep(pencils, 0, norm_gains[1], qkv_weight[1], out_weight[1], meridian), state, 1)

    def column_steps(pencils):
        pencils = sweep(pencils, 2, norm_gains[2], qkv_weight[2], out_weight[2], column)
        return feed_forward(pencils, norm_gains[3], mlp_in, mlp_out)
    return in_groups(column_steps, state, 0)
```

```python
import math

import jax
import jax.numpy as jnp
from jax import lax
from jax.experimental import pallas as pl
from jax.experimental.pallas import tpu as pltpu
from jax.sharding import PartitionSpec as P

D = 768
HALF = D // 2
HEADS = 12
PAIRS = HEADS // 2
FF = 3072
LEV = 4
EPS = 1e-06
LOG2E = math.log2(math.e)
SCALE = 0.125 * LOG2E
OUTSIDE = -1e30
MIB = 1 << 20
BF = jnp.bfloat16
F32 = jnp.float32


def dot(a, b):
    return lax.dot_general(a, b, (((1,), (0,)), ((), ())), preferred_element_type=F32)


def dot_t(a, b):
    return lax.dot_general(a, b, (((1,), (1,)), ((), ())), preferred_element_type=F32)


def one_hot(rows, cols, target):
    row = lax.broadcasted_iota(jnp.int32, (rows, cols), 0)
    col = lax.broadcasted_iota(jnp.int32, (rows, cols), 1)
    return jnp.where(target(row) == col, 1.0, 0.0).astype(F32).astype(BF)


def normalize(x, gain):
    square = jnp.mean(x * x, axis=-1, keepdims=True)
    return (x * lax.rsqrt(square + EPS) * gain).astype(BF)


def head_masks():
    lane = lax.broadcasted_iota(jnp.int32, (1, 128), 1)
    even = jnp.where(lane < 64, 1.0, 0.0)
    return even.astype(BF), (1.0 - even).astype(BF)


def toeplitz(row, count):
    wide = jnp.broadcast_to(row * LOG2E, (count, 256))
    return pltpu.roll(wide, 0, 1, stride=1, stride_axis=0)


def attend_pair(q, k, v, bias_even, bias_odd):
    even, odd = head_masks()
    count = k.shape[0]
    weights = []
    for mask, bias in ((even, bias_even), (odd, bias_odd)):
        scores = dot_t(q * mask, k) * SCALE + bias
        top = jnp.max(scores, axis=-1, keepdims=True)
        weights.append(jnp.exp2(scores - top).astype(BF))
    ones = [jnp.broadcast_to(mask, (count, 128)) for mask in (even, odd)]
    values = jnp.concatenate(
        [
            jnp.concatenate([v * even, ones[0]], axis=1),
            jnp.concatenate([v * odd, ones[1]], axis=1),
        ],
        axis=0,
    )
    total = dot(jnp.concatenate(weights, axis=1), values)
    return (total[:, :128] / total[:, 128:]).astype(BF)


def pack_kernel(fields_ref, first_ref, second_ref):
    for block in range(4):
        x = fields_ref[16 * block : 16 * block + 16].reshape(256, D).astype(BF)
        stacked = jnp.concatenate([x[:, :HALF], x[:, HALF:]], axis=0)
        for pair, out_ref in enumerate((first_ref, second_ref)):
            move = one_hot(
                256,
                512,
                lambda r: (r // 4) % 2 * 256 + r // 16 * 16 + r % 4 * 4 + 2 * pair + r // 8 % 2,
            )
            out_ref[256 * block : 256 * block + 256] = dot(move, stacked).astype(BF)


def longitude_kernel(x_ref, gains_ref, qkv_w_ref, out_w_ref, bias_ref, out_ref, state, qkv, attended):
    low = one_hot(128, 256, lambda t: t // 4 * 8 + t % 4)
    high = one_hot(128, 256, lambda t: t // 4 * 8 + 4 + t % 4)
    for block in range(4):
        rows = x_ref[256 * block : 256 * block + 256]
        state[128 * block : 128 * block + 128, :HALF] = dot(low, rows)
        state[128 * block : 128 * block + 128, HALF:] = dot(high, rows)
    normed = normalize(state[...], gains_ref[0:1])
    qkv[...] = dot(normed, qkv_w_ref[0]).astype(BF)
    for pair in range(PAIRS):
        bias = [toeplitz(bias_ref[2 * pair + e : 2 * pair + e + 1], 256) for e in range(2)]
        cols = [slice(m * D + 128 * pair, m * D + 128 * pair + 128) for m in range(3)]
        for pencil in range(2):
            rows = slice(256 * pencil, 256 * pencil + 256)
            attended[rows, 128 * pair : 128 * pair + 128] = attend_pair(
                qkv[rows, cols[0]], qkv[rows, cols[1]], qkv[rows, cols[2]], bias[0], bias[1]
            )
    update = (state[...] + dot(attended[...], out_w_ref[0])).astype(BF)
    for block in range(4):
        tokens = jnp.concatenate(
            [update[64 * block : 64 * block + 64], update[256 + 64 * block : 320 + 64 * block]], axis=0
        )
        stacked = jnp.concatenate([tokens[:, :HALF], tokens[:, HALF:]], axis=0)
        for lat in range(2):
            move = one_hot(
                128,
                256,
                lambda r: r // 4 % 2 * 128 + r // 2 % 2 * 64 + r // 8 * 4 + 2 * lat + r % 2,
            )
            start = 512 * lat + 128 * block
            out_ref[start : start + 128] = dot(move, stacked).astype(BF)


def attend_blocks(qkv, attended, bias_ref, blocks):
    for pair in range(PAIRS):
        bias = [
            toeplitz(bias_ref[2 * pair + e : 2 * pair + e + 1], 128)[:, :128] for e in range(2)
        ]
        cols = [slice(m * D + 128 * pair, m * D + 128 * pair + 128) for m in range(3)]
        for pieces in blocks:
            q, k, v = (
                jnp.concatenate([qkv[piece, col] for piece in pieces], axis=0) for col in cols
            )
            result = attend_pair(q, k, v, bias[0], bias[1])
            at = 0
            for piece in pieces:
                size = piece.stop - piece.start
                attended[piece, 128 * pair : 128 * pair + 128] = result[at : at + size]
                at += size


def latitude_kernel(
    lat_ref, x_ref, gains_ref, qkv_w_ref, out_w_ref, bias_ref, own_ref, other_ref, state, qkv, attended
):
    moves = [
        one_hot(
            128,
            256,
            lambda t: (t % 16 * 2 + t // 32 % 2) * 8 + half * 4 + t // 16 % 2 * 2 + t // 64,
        )
        for half in range(2)
    ]
    for block in range(4):
        rows = x_ref[256 * block : 256 * block + 256]
        for half in range(2):
            moved = dot(moves[half], rows)
            for group in range(8):
                start = 64 * group + 16 * block
                state[start : start + 16, HALF * half : HALF * half + HALF] = moved[
                    16 * group : 16 * group + 16
                ]
    normed = normalize(state[...], gains_ref[1:2])
    qkv[...] = dot(normed, qkv_w_ref[0]).astype(BF)
    attend_blocks(qkv, attended, bias_ref, [[slice(128 * n, 128 * n + 128)] for n in range(4)])
    state[...] = state[...] + dot(attended[...], out_w_ref[0])
    lat = lat_ref[0]
    for pencil in range(4):
        start = pl.multiple_of(128 * pencil + 64 * lat, 64)
        own_ref[pencil] = state[pl.ds(start, 64)]
        start = pl.multiple_of(128 * pencil + 64 * (1 - lat), 64)
        other_ref[pencil] = state[pl.ds(start, 64)].astype(BF)


def column_kernel(
    place_ref,
    first_ref,
    second_ref,
    gains_ref,
    qkv_w_ref,
    out_w_ref,
    bias_ref,
    in_w_ref,
    mlp_w_ref,
    *rest,
):
    out_ref, state, qkv, attended = rest[-4:]
    state[0:256] = first_ref[...].reshape(256, D).astype(F32)
    state[256:512] = second_ref[...].reshape(256, D).astype(F32)
    normed = normalize(state[...], gains_ref[2:3])
    qkv[...] = dot(normed, qkv_w_ref[0]).astype(BF)
    blocks = []
    for lon in range(2):
        for part in range(2):
            starts = [256 * c + 64 * (2 * lon + v) + 32 * part for c in range(2) for v in range(2)]
            blocks.append([slice(s, s + 32) for s in starts])
    attend_blocks(qkv, attended, bias_ref, blocks)
    state[...] = state[...] + dot(attended[...], out_w_ref[0])
    normed = normalize(state[...], gains_ref[3:4])
    total = state[...]
    for part in range(4):
        cols = slice(FF // 4 * part, FF // 4 * (part + 1))
        u = dot(normed, in_w_ref[:, cols])
        bend = u * (math.sqrt(2 / math.pi) + (math.sqrt(2 / math.pi) * 0.044715) * (u * u))
        hidden = (0.5 * u * (1.0 + jnp.tanh(bend))).astype(BF)
        total = total + dot(hidden, mlp_w_ref[cols])
    for lon in range(2):
        for lev in range(LEV):
            start = 256 * (lev // 2) + 64 * (2 * lon + lev % 2)
            out_ref[:, 0, lon, lev, :] = total[start : start + 64]


def whole(shape=None):
    return pl.BlockSpec(memory_space=pltpu.VMEM)


def weight_spec(rows, cols, member):
    return pl.BlockSpec((1, rows, cols), lambda *_: (member, 0, 0), pipeline_mode=pl.Buffered(1))


def full_spec(*shape):
    return pl.BlockSpec(shape, lambda *_: (0,) * len(shape), pipeline_mode=pl.Buffered(1))


def params(mib):
    return pltpu.CompilerParams(vmem_limit_bytes=mib * MIB)


def scratch():
    return [
        pltpu.VMEM((512, D), F32),
        pltpu.VMEM((512, 3 * D), BF),
        pltpu.VMEM((512, D), BF),
    ]


def pack(fields):
    return pl.pallas_call(
        pack_kernel,
        out_shape=[jax.ShapeDtypeStruct((1024, HALF), BF)] * 2,
        compiler_params=params(32),
        name="pack",
    )(fields)


def longitude(x, gains, qkv_w, out_w, bias):
    return pl.pallas_call(
        longitude_kernel,
        grid=(1,),
        in_specs=[
            full_spec(1024, HALF),
            full_spec(4, D),
            weight_spec(D, 3 * D, 0),
            weight_spec(D, D, 0),
            full_spec(HEADS, 256),
        ],
        out_specs=full_spec(1024, HALF),
        out_shape=jax.ShapeDtypeStruct((1024, HALF), BF),
        scratch_shapes=scratch(),
        compiler_params=params(40),
        name="longitude",
    )(x, gains, qkv_w, out_w, bias)


def latitude(lat, x, gains, qkv_w, out_w, bias):
    return pl.pallas_call(
        latitude_kernel,
        grid_spec=pltpu.PrefetchScalarGridSpec(
            num_scalar_prefetch=1,
            grid=(1,),
            in_specs=[
                full_spec(1024, HALF),
                full_spec(4, D),
                weight_spec(D, 3 * D, 1),
                weight_spec(D, D, 1),
                full_spec(HEADS, 256),
            ],
            out_specs=[full_spec(4, 64, D), full_spec(4, 64, D)],
            scratch_shapes=scratch(),
        ),
        out_shape=[
            jax.ShapeDtypeStruct((4, 64, D), F32),
            jax.ShapeDtypeStruct((4, 64, D), BF),
        ],
        compiler_params=params(40),
        name="latitude",
    )(lat, x, gains, qkv_w, out_w, bias)


def column(place, first, second, gains, qkv_w, out_w, bias, mlp_in, mlp_out, out=None):
    in_specs = [
        full_spec(4, 64, D),
        full_spec(4, 64, D),
        full_spec(4, D),
        weight_spec(D, 3 * D, 2),
        weight_spec(D, D, 2),
        full_spec(HEADS, 256),
        full_spec(D, FF),
        full_spec(FF, D),
    ]
    operands = [place, first, second, gains, qkv_w, out_w, bias, mlp_in, mlp_out]
    aliases = {}
    if out is not None:
        in_specs.append(pl.BlockSpec(memory_space=pl.ANY))
        operands.append(out)
        aliases = {len(operands) - 1: 0}
    return pl.pallas_call(
        column_kernel,
        grid_spec=pltpu.PrefetchScalarGridSpec(
            num_scalar_prefetch=1,
            grid=(1,),
            in_specs=in_specs,
            out_specs=pl.BlockSpec(
                (64, 1, 2, LEV, D),
                lambda _, place_ref: (0, place_ref[0], 0, 0, 0),
                pipeline_mode=pl.Buffered(1),
            ),
            scratch_shapes=scratch(),
        ),
        out_shape=jax.ShapeDtypeStruct((64, 2, 2, LEV, D), F32),
        input_output_aliases=aliases,
        compiler_params=params(56),
        name="column",
    )(*operands)


def per_device(
    fields,
    norm_gains,
    qkv_weight,
    out_weight,
    longitude_bias,
    latitude_bias,
    level_bias,
    mlp_in,
    mlp_out,
):
    axes = ("lat", "lon")
    spot = lax.axis_index("lat").astype(jnp.int32).reshape(1)
    latitude_row = jnp.concatenate(
        [latitude_bias[:, 127:], jnp.zeros((HEADS, 1), F32), latitude_bias[:, :127]], axis=1
    )
    offsets = jnp.concatenate([level_bias[:, 3:], jnp.zeros((HEADS, 1), F32), level_bias[:, :3]], axis=1)
    level_row = jnp.concatenate(
        [offsets[:, :, None], jnp.full((HEADS, 8, 31), OUTSIDE, F32)], axis=2
    ).reshape(HEADS, 256)

    def exchange(x):
        return lax.all_to_all(
            x.reshape(128, 8, HALF), axes, split_axis=0, concat_axis=0, tiled=True
        ).reshape(1024, HALF)

    circles = [exchange(x) for x in pack(fields)]
    meridians = [
        exchange(longitude(x, norm_gains, qkv_weight, out_weight, longitude_bias)) for x in circles
    ]
    own, other = [], []
    for x in meridians:
        kept, sent = latitude(spot, x, norm_gains, qkv_weight, out_weight, latitude_row)
        own.append(kept)
        other.append(lax.ppermute(sent, "lat", [(0, 1), (1, 0)]))
    rest = (norm_gains, qkv_weight, out_weight, level_row, mlp_in, mlp_out)
    out = column(spot, *own, *rest)
    out = column(1 - spot, *other, *rest, out=out)
    return out.reshape(64, 4, LEV, D)


def solution(mesh):
    in_specs = (P("lat", "lon", None, None), P(), P(), P(), P(), P(), P(), P(), P())
    out_specs = P("lat", "lon", None, None)
    return jax.shard_map(
        per_device, mesh=mesh, in_specs=in_specs, out_specs=out_specs, check_vma=False
    )
```

```python
import math

import jax
import jax.numpy as jnp
from jax import lax
from jax.experimental import pallas as pl
from jax.experimental.pallas import tpu as pltpu
from jax.sharding import PartitionSpec as P

D = 768
HALF = D // 2
HEADS = 12
PAIRS = HEADS // 2
FF = 3072
LEV = 4
EPS = 1e-06
LOG2E = math.log2(math.e)
SCALE = 0.125 * LOG2E
OUTSIDE = -1e30
MIB = 1 << 20
BF = jnp.bfloat16
F32 = jnp.float32


def dot(a, b):
    return lax.dot_general(a, b, (((1,), (0,)), ((), ())), preferred_element_type=F32)


def dot_t(a, b):
    return lax.dot_general(a, b, (((1,), (1,)), ((), ())), preferred_element_type=F32)


def one_hot(rows, cols, target):
    row = lax.broadcasted_iota(jnp.int32, (rows, cols), 0)
    col = lax.broadcasted_iota(jnp.int32, (rows, cols), 1)
    return jnp.where(target(row) == col, 1.0, 0.0).astype(F32).astype(BF)


def normalize(x, gain):
    square = jnp.mean(x * x, axis=-1, keepdims=True)
    return (x * lax.rsqrt(square + EPS) * gain).astype(BF)


def head_masks():
    lane = lax.broadcasted_iota(jnp.int32, (1, 128), 1)
    even = jnp.where(lane < 64, 1.0, 0.0)
    return even.astype(BF), (1.0 - even).astype(BF)


def toeplitz(row, count):
    wide = jnp.broadcast_to(row * LOG2E, (count, 256))
    return pltpu.roll(wide, 0, 1, stride=1, stride_axis=0)


def attend_pair(q, k, v, bias):
    even, odd = head_masks()
    rows, count = q.shape[0], k.shape[0]
    scores = dot_t(jnp.concatenate([q * even, q * odd], axis=0), k) * SCALE + bias
    top = jnp.max(scores, axis=-1, keepdims=True)
    weights = jnp.exp2(scores - top).astype(BF)
    ones = [jnp.broadcast_to(mask, (count, 128)) for mask in (even, odd)]
    values = jnp.concatenate(
        [
            jnp.concatenate([v * even, ones[0]], axis=1),
            jnp.concatenate([v * odd, ones[1]], axis=1),
        ],
        axis=0,
    )
    total = dot(jnp.concatenate([weights[:rows], weights[rows:]], axis=1), values)
    return (total[:, :128] / total[:, 128:]).astype(BF)


def fetch(source, target, sem):
    copy = pltpu.make_async_copy(source, target, sem)
    copy.start()
    return copy


def pack_kernel(fields_ref, out_ref, x, y, in_sems, out_sems):
    move = one_hot(128, 128, lambda r: r // 16 * 16 + r % 4 * 4 + r // 4 % 4)
    loads = [
        fetch(fields_ref.at[pl.ds(8 * n, 8)], x.at[pl.ds(8 * n, 8)], in_sems.at[n]) for n in range(8)
    ]
    stores = []
    for n in range(8):
        loads[n].wait()
        rows = pl.ds(128 * n, 128)
        y[rows] = dot(move, x[8 * n : 8 * n + 8].reshape(128, D).astype(BF)).astype(BF)
        stores.append(fetch(y.at[rows], out_ref.at[rows], out_sems.at[n]))
    for store in stores:
        store.wait()


def tables_kernel(lon_ref, lat_ref, lev_ref, lon_out, lat_out, lev_out):
    for head in range(HEADS):
        pair, rows = head // 2, 256 * (head % 2)
        lon_out[pair, rows : rows + 256] = toeplitz(lon_ref[head : head + 1], 256)
        rows = 128 * (head % 2)
        lat_out[pair, rows : rows + 128] = toeplitz(lat_ref[head : head + 1], 128)[:, :128]
        lev_out[pair, rows : rows + 128] = toeplitz(lev_ref[head : head + 1], 128)[:, :128]


def fetch_weights(qkv_w_hbm, out_w_hbm, qkv_w, out_w, sems, member):
    copies = [
        fetch(
            qkv_w_hbm.at[member, :, pl.ds(D * n, D)], qkv_w.at[:, pl.ds(D * n, D)], sems.at[n]
        )
        for n in range(3)
    ]
    return copies + [fetch(out_w_hbm.at[member], out_w, sems.at[3])]


def project(normed, qkv_w, qkv, copies):
    for n in range(3):
        copies[n].wait()
        cols = slice(D * n, D * n + D)
        qkv[:, cols] = dot(normed, qkv_w[:, cols]).astype(BF)


def longitude_kernel(
    x_ref,
    gains_ref,
    qkv_w_hbm,
    out_w_hbm,
    bias_hbm,
    out_hbm,
    x,
    bias,
    qkv_w,
    out_w,
    state,
    qkv,
    attended,
    bias_sems,
    w_sems,
    out_sems,
):
    weights = fetch_weights(qkv_w_hbm, out_w_hbm, qkv_w, out_w, w_sems, 0)
    tables = [fetch(bias_hbm.at[n], bias.at[n], bias_sems.at[n]) for n in range(PAIRS)]
    move = one_hot(128, 128, lambda t: t % 64 // 4 * 8 + t // 64 * 4 + t % 4)
    for block in range(8):
        moved = dot(move, x_ref[128 * block : 128 * block + 128])
        for level in range(2):
            start = 512 * (block // 4) + 256 * level + 64 * (block % 4)
            state[start : start + 64] = moved[64 * level : 64 * level + 64]
    project(normalize(state[...], gains_ref[0:1]), qkv_w, qkv, weights)
    for pair in range(PAIRS):
        tables[pair].wait()
        cols = [slice(m * D + 128 * pair, m * D + 128 * pair + 128) for m in range(3)]
        for pencil in range(4):
            rows = slice(256 * pencil, 256 * pencil + 256)
            attended[rows, 128 * pair : 128 * pair + 128] = attend_pair(
                qkv[rows, cols[0]], qkv[rows, cols[1]], qkv[rows, cols[2]], bias[pair]
            )
    weights[3].wait()
    x[...] = (state[...] + dot(attended[...], out_w[...])).astype(BF)
    move = one_hot(
        128,
        128,
        lambda r: r // 2 % 4 * 32 + r // 8 % 8 * 4 + r // 64 * 2 + r % 2,
    )
    stores = []
    for block in range(8):
        tokens = jnp.concatenate(
            [x[256 * n + 32 * block : 256 * n + 32 * block + 32] for n in range(4)], axis=0
        )
        moved = dot(move, tokens).astype(BF)
        for lat in range(2):
            rows = pl.ds(512 * lat + 64 * block, 64)
            attended[rows] = moved[64 * lat : 64 * lat + 64]
            stores.append(fetch(attended.at[rows], out_hbm.at[rows], out_sems.at[2 * block + lat]))
    for store in stores:
        store.wait()


def attend_blocks(qkv, attended, bias_ref, blocks):
    for pair in range(PAIRS):
        cols = [slice(m * D + 128 * pair, m * D + 128 * pair + 128) for m in range(3)]
        for pieces in blocks:
            q, k, v = (
                jnp.concatenate([qkv[piece, col] for piece in pieces], axis=0) for col in cols
            )
            result = attend_pair(q, k, v, bias_ref[pair])
            at = 0
            for piece in pieces:
                size = piece.stop - piece.start
                attended[piece, 128 * pair : 128 * pair + 128] = result[at : at + size]
                at += size


def latitude_kernel(
    member,
    lat_ref,
    x_ref,
    gains_ref,
    qkv_w_hbm,
    out_w_hbm,
    bias_hbm,
    own_ref,
    other_ref,
    bias,
    qkv_w,
    out_w,
    state,
    qkv,
    attended,
    w_sems,
    bias_sem,
):
    weights = fetch_weights(qkv_w_hbm, out_w_hbm, qkv_w, out_w, w_sems, 1)
    table = fetch(bias_hbm, bias, bias_sem)
    move = one_hot(
        64,
        128,
        lambda t: t % 8 * 16 + t // 32 * 8 + t // 8 % 2 * 4 + t // 16 % 2 * 2 + member,
    )
    for block in range(8):
        moved = dot(move, x_ref[128 * block : 128 * block + 128])
        for group in range(8):
            start = 64 * group + 8 * block
            state[start : start + 8] = moved[8 * group : 8 * group + 8]
    project(normalize(state[...], gains_ref[1:2]), qkv_w, qkv, weights)
    table.wait()
    attend_blocks(qkv, attended, bias, [[slice(128 * n, 128 * n + 128)] for n in range(4)])
    weights[3].wait()
    state[...] = state[...] + dot(attended[...], out_w[...])
    lat = lat_ref[0]
    for pencil in range(4):
        start = pl.multiple_of(128 * pencil + 64 * lat, 64)
        own_ref[pencil] = state[pl.ds(start, 64)]
        start = pl.multiple_of(128 * pencil + 64 * (1 - lat), 64)
        other_ref[pencil] = state[pl.ds(start, 64)].astype(BF)


def column_kernel(
    place_ref,
    first_ref,
    second_ref,
    gains_ref,
    qkv_w_hbm,
    out_w_hbm,
    bias_hbm,
    in_w_hbm,
    mlp_w_hbm,
    *rest,
):
    out_ref, bias, qkv_w, out_w, in_w, mlp_w, state, qkv, attended, w_sems, mlp_sems, bias_sem = rest[-12:]
    weights = fetch_weights(qkv_w_hbm, out_w_hbm, qkv_w, out_w, w_sems, 2)
    table = fetch(bias_hbm, bias, bias_sem)
    parts = [pl.ds(FF // 4 * n, FF // 4) for n in range(4)]
    into = [fetch(in_w_hbm.at[:, part], in_w.at[:, part], mlp_sems.at[0, n]) for n, part in enumerate(parts)]
    back = [fetch(mlp_w_hbm.at[part], mlp_w.at[part], mlp_sems.at[1, n]) for n, part in enumerate(parts)]
    state[0:256] = first_ref[...].reshape(256, D).astype(F32)
    state[256:512] = second_ref[...].reshape(256, D).astype(F32)
    project(normalize(state[...], gains_ref[2:3]), qkv_w, qkv, weights)
    blocks = []
    for lon in range(2):
        for part in range(2):
            starts = [256 * lon + 64 * lev + 32 * part for lev in range(LEV)]
            blocks.append([slice(s, s + 32) for s in starts])
    table.wait()
    attend_blocks(qkv, attended, bias, blocks)
    weights[3].wait()
    state[...] = state[...] + dot(attended[...], out_w[...])
    normed = normalize(state[...], gains_ref[3:4])
    total = state[...]
    for n in range(4):
        cols = slice(FF // 4 * n, FF // 4 * (n + 1))
        into[n].wait()
        u = dot(normed, in_w[:, cols])
        bend = u * (math.sqrt(2 / math.pi) + (math.sqrt(2 / math.pi) * 0.044715) * (u * u))
        hidden = (0.5 * u * (1.0 + jnp.tanh(bend))).astype(BF)
        back[n].wait()
        total = total + dot(hidden, mlp_w[cols])
    for lon in range(2):
        for lev in range(LEV):
            start = 256 * lon + 64 * lev
            out_ref[:, 0, lon, lev, :] = total[start : start + 64]


IN_VMEM = pl.BlockSpec(memory_space=pltpu.VMEM)
IN_HBM = pl.BlockSpec(memory_space=pltpu.HBM)
ANYWHERE = pl.BlockSpec(memory_space=pl.ANY)
DMA = pltpu.SemaphoreType.DMA


def in_hbm(*arrays):
    return [pltpu.with_memory_space_constraint(x, pltpu.HBM) for x in arrays]


def params(mib):
    return pltpu.CompilerParams(vmem_limit_bytes=mib * MIB)


def scratch(tokens):
    return [
        pltpu.VMEM((D, 3 * D), BF),
        pltpu.VMEM((D, D), BF),
        pltpu.VMEM((tokens, D), F32),
        pltpu.VMEM((tokens, 3 * D), BF),
        pltpu.VMEM((tokens, D), BF),
    ]


def pack(fields):
    return pl.pallas_call(
        pack_kernel,
        in_specs=[IN_HBM],
        out_specs=IN_HBM,
        out_shape=pltpu.HBM((1024, D), BF),
        scratch_shapes=[
            pltpu.VMEM((64, 4, LEV, D), F32),
            pltpu.VMEM((1024, D), BF),
            DMA((8,)),
            DMA((8,)),
        ],
        compiler_params=params(16),
        name="pack",
    )(*in_hbm(fields))


def tables(lon_row, lat_row, lev_row):
    return pl.pallas_call(
        tables_kernel,
        in_specs=[IN_VMEM] * 3,
        out_shape=[
            pltpu.HBM((PAIRS, 512, 256), F32),
            pltpu.HBM((PAIRS, 256, 128), F32),
            pltpu.HBM((PAIRS, 256, 128), F32),
        ],
        compiler_params=params(16),
        name="tables",
    )(lon_row, lat_row, lev_row)


def longitude(x, gains, qkv_w, out_w, bias):
    return pl.pallas_call(
        longitude_kernel,
        in_specs=[IN_VMEM] * 2 + [ANYWHERE] * 3,
        out_specs=IN_HBM,
        out_shape=pltpu.HBM((1024, D), BF),
        scratch_shapes=[
            pltpu.VMEM((1024, D), BF),
            pltpu.VMEM((PAIRS, 512, 256), F32),
            *scratch(1024),
            DMA((PAIRS,)),
            DMA((4,)),
            DMA((16,)),
        ],
        compiler_params=params(40),
        name="longitude",
    )(x, gains, *in_hbm(qkv_w, out_w, bias))


def latitude(member, lat, x, gains, qkv_w, out_w, bias):
    return pl.pallas_call(
        lambda *refs: latitude_kernel(member, *refs),
        in_specs=[pl.BlockSpec(memory_space=pltpu.SMEM)] + [IN_VMEM] * 2 + [ANYWHERE] * 3,
        out_specs=[IN_VMEM, IN_VMEM],
        out_shape=[
            jax.ShapeDtypeStruct((4, 64, D), F32),
            jax.ShapeDtypeStruct((4, 64, D), BF),
        ],
        scratch_shapes=[
            pltpu.VMEM((PAIRS, 256, 128), F32),
            *scratch(512),
            DMA((4,)),
            DMA(()),
        ],
        compiler_params=params(32),
        name="latitude",
    )(lat, x, gains, *in_hbm(qkv_w, out_w, bias))


def column(place, first, second, gains, qkv_w, out_w, bias, mlp_in, mlp_out, out=None):
    in_specs = [IN_VMEM] * 3 + [ANYWHERE] * 5
    operands = [place, first, second, gains, *in_hbm(qkv_w, out_w, bias, mlp_in, mlp_out)]
    aliases = {}
    if out is not None:
        in_specs.append(ANYWHERE)
        operands.append(out)
        aliases = {len(operands) - 1: 0}
    return pl.pallas_call(
        column_kernel,
        grid_spec=pltpu.PrefetchScalarGridSpec(
            num_scalar_prefetch=1,
            grid=(1,),
            in_specs=in_specs,
            out_specs=pl.BlockSpec(
                (64, 1, 2, LEV, D),
                lambda _, place_ref: (0, place_ref[0], 0, 0, 0),
                pipeline_mode=pl.Buffered(1),
            ),
            scratch_shapes=[
                pltpu.VMEM((PAIRS, 256, 128), F32),
                pltpu.VMEM((D, 3 * D), BF),
                pltpu.VMEM((D, D), BF),
                pltpu.VMEM((D, FF), BF),
                pltpu.VMEM((FF, D), BF),
                pltpu.VMEM((512, D), F32),
                pltpu.VMEM((512, 3 * D), BF),
                pltpu.VMEM((512, D), BF),
                DMA((4,)),
                DMA((2, 4)),
                DMA(()),
            ],
        ),
        out_shape=jax.ShapeDtypeStruct((64, 2, 2, LEV, D), F32),
        input_output_aliases=aliases,
        compiler_params=params(48),
        name="column",
    )(*operands)


def per_device(
    fields,
    norm_gains,
    qkv_weight,
    out_weight,
    longitude_bias,
    latitude_bias,
    level_bias,
    mlp_in,
    mlp_out,
):
    axes = ("lat", "lon")
    spot = lax.axis_index("lat").astype(jnp.int32).reshape(1)
    latitude_row = jnp.concatenate(
        [latitude_bias[:, 127:], jnp.zeros((HEADS, 1), F32), latitude_bias[:, :127]], axis=1
    )
    offsets = jnp.concatenate([level_bias[:, 3:], jnp.zeros((HEADS, 1), F32), level_bias[:, :3]], axis=1)
    level_row = jnp.concatenate(
        [offsets[:, :, None], jnp.full((HEADS, 8, 31), OUTSIDE, F32)], axis=2
    ).reshape(HEADS, 256)

    def exchange(x):
        return lax.all_to_all(
            x.reshape(128, 8, D), axes, split_axis=0, concat_axis=0, tiled=True
        ).reshape(1024, D)

    circles = exchange(pack(fields))
    lon_table, lat_table, lev_table = tables(longitude_bias, latitude_row, level_row)
    meridians = exchange(longitude(circles, norm_gains, qkv_weight, out_weight, lon_table))
    own, other = [], []
    for member in range(2):
        kept, sent = latitude(member, spot, meridians, norm_gains, qkv_weight, out_weight, lat_table)
        own.append(kept)
        other.append(lax.ppermute(sent, "lat", [(0, 1), (1, 0)]))
    rest = (norm_gains, qkv_weight, out_weight, lev_table, mlp_in, mlp_out)
    out = column(spot, *own, *rest)
    out = column(1 - spot, *other, *rest, out=out)
    return out.reshape(64, 4, LEV, D)


def solution(mesh):
    in_specs = (P("lat", "lon", None, None), P(), P(), P(), P(), P(), P(), P(), P())
    out_specs = P("lat", "lon", None, None)
    return jax.shard_map(
        per_device, mesh=mesh, in_specs=in_specs, out_specs=out_specs, check_vma=False
    )
```

```python
import math

import jax
import jax.numpy as jnp
from jax import lax
from jax.experimental import pallas as pl
from jax.experimental.pallas import tpu as pltpu
from jax.sharding import PartitionSpec as P

D = 768
HALF = D // 2
HEADS = 12
PAIRS = HEADS // 2
FF = 3072
LEV = 4
EPS = 1e-06
LOG2E = math.log2(math.e)
SCALE = 0.125 * LOG2E
OUTSIDE = -1e30
MIB = 1 << 20
BF = jnp.bfloat16
F32 = jnp.float32


def dot(a, b):
    return lax.dot_general(a, b, (((1,), (0,)), ((), ())), preferred_element_type=F32)


def dot_t(a, b):
    return lax.dot_general(a, b, (((1,), (1,)), ((), ())), preferred_element_type=F32)


def one_hot(rows, cols, target):
    row = lax.broadcasted_iota(jnp.int32, (rows, cols), 0)
    col = lax.broadcasted_iota(jnp.int32, (rows, cols), 1)
    return jnp.where(target(row) == col, 1.0, 0.0).astype(F32).astype(BF)


def normalize(x, gain):
    square = jnp.mean(x * x, axis=-1, keepdims=True)
    return (x * lax.rsqrt(square + EPS) * gain).astype(BF)


def head_masks():
    lane = lax.broadcasted_iota(jnp.int32, (1, 128), 1)
    even = jnp.where(lane < 64, 1.0, 0.0)
    return even.astype(BF), (1.0 - even).astype(BF)


def toeplitz(row, count):
    wide = jnp.broadcast_to(row * LOG2E, (count, 256))
    return pltpu.roll(wide, 0, 1, stride=1, stride_axis=0)


def attend_pair(q, k, v, bias):
    even, odd = head_masks()
    rows, count = q.shape[0], k.shape[0]
    scores = dot_t(jnp.concatenate([q * even, q * odd], axis=0), k) * SCALE + bias
    top = jnp.max(scores, axis=-1, keepdims=True)
    weights = jnp.exp2(scores - top).astype(BF)
    ones = [jnp.broadcast_to(mask, (count, 128)) for mask in (even, odd)]
    values = jnp.concatenate(
        [
            jnp.concatenate([v * even, ones[0]], axis=1),
            jnp.concatenate([v * odd, ones[1]], axis=1),
        ],
        axis=0,
    )
    total = dot(jnp.concatenate([weights[:rows], weights[rows:]], axis=1), values)
    return (total[:, :128] / total[:, 128:]).astype(BF)


def fetch(source, target, sem):
    copy = pltpu.make_async_copy(source, target, sem)
    copy.start()
    return copy


def pack_kernel(fields_ref, out_ref, x, y, in_sems, out_sems):
    move = one_hot(128, 128, lambda r: r // 16 * 16 + r % 4 * 4 + r // 4 % 4)
    loads = [
        fetch(fields_ref.at[pl.ds(8 * n, 8)], x.at[pl.ds(8 * n, 8)], in_sems.at[n]) for n in range(8)
    ]
    stores = []
    for n in range(8):
        loads[n].wait()
        rows = pl.ds(128 * n, 128)
        y[rows] = dot(move, x[8 * n : 8 * n + 8].reshape(128, D).astype(BF)).astype(BF)
        stores.append(fetch(y.at[rows], out_ref.at[rows], out_sems.at[n]))
    for store in stores:
        store.wait()


def tables_kernel(lon_ref, lat_ref, lev_ref, lon_out, lat_out, lev_out):
    for head in range(HEADS):
        pair, rows = head // 2, 256 * (head % 2)
        lon_out[pair, rows : rows + 256] = toeplitz(lon_ref[head : head + 1], 256)
        rows = 128 * (head % 2)
        lat_out[pair, rows : rows + 128] = toeplitz(lat_ref[head : head + 1], 128)[:, :128]
        lev_out[pair, rows : rows + 128] = toeplitz(lev_ref[head : head + 1], 128)[:, :128]


def fetch_weights(qkv_w_hbm, out_w_hbm, qkv_w, out_w, sems, member):
    copies = [
        fetch(
            qkv_w_hbm.at[member, :, pl.ds(D * n, D)], qkv_w.at[:, pl.ds(D * n, D)], sems.at[n]
        )
        for n in range(3)
    ]
    return copies + [fetch(out_w_hbm.at[member], out_w, sems.at[3])]


def project(normed, qkv_w, qkv, copies):
    for n in range(3):
        copies[n].wait()
        cols = slice(D * n, D * n + D)
        qkv[:, cols] = dot(normed, qkv_w[:, cols]).astype(BF)


def longitude_kernel(
    x_ref,
    gains_ref,
    qkv_w_hbm,
    out_w_hbm,
    bias_hbm,
    out_hbm,
    x,
    bias,
    qkv_w,
    out_w,
    state,
    qkv,
    attended,
    bias_sems,
    w_sems,
    out_sems,
):
    weights = fetch_weights(qkv_w_hbm, out_w_hbm, qkv_w, out_w, w_sems, 0)
    tables = [fetch(bias_hbm.at[n], bias.at[n], bias_sems.at[n]) for n in range(PAIRS)]
    move = one_hot(128, 128, lambda t: t % 64 // 4 * 8 + t // 64 * 4 + t % 4)
    for block in range(8):
        moved = dot(move, x_ref[128 * block : 128 * block + 128])
        for level in range(2):
            start = 512 * (block // 4) + 256 * level + 64 * (block % 4)
            state[start : start + 64] = moved[64 * level : 64 * level + 64]
    project(normalize(state[...], gains_ref[0:1]), qkv_w, qkv, weights)
    for pair in range(PAIRS):
        tables[pair].wait()
        cols = [slice(m * D + 128 * pair, m * D + 128 * pair + 128) for m in range(3)]
        for pencil in range(4):
            rows = slice(256 * pencil, 256 * pencil + 256)
            attended[rows, 128 * pair : 128 * pair + 128] = attend_pair(
                qkv[rows, cols[0]], qkv[rows, cols[1]], qkv[rows, cols[2]], bias[pair]
            )
    weights[3].wait()
    x[...] = (state[...] + dot(attended[...], out_w[...])).astype(BF)
    move = one_hot(
        128,
        128,
        lambda r: r // 2 % 4 * 32 + r // 8 % 8 * 4 + r // 64 * 2 + r % 2,
    )
    stores = []
    for block in range(8):
        tokens = jnp.concatenate(
            [x[256 * n + 32 * block : 256 * n + 32 * block + 32] for n in range(4)], axis=0
        )
        moved = dot(move, tokens).astype(BF)
        for lat in range(2):
            rows = pl.ds(512 * lat + 64 * block, 64)
            attended[rows] = moved[64 * lat : 64 * lat + 64]
            stores.append(fetch(attended.at[rows], out_hbm.at[rows], out_sems.at[2 * block + lat]))
    for store in stores:
        store.wait()


def attend_blocks(qkv, attended, bias_ref, blocks):
    for pair in range(PAIRS):
        cols = [slice(m * D + 128 * pair, m * D + 128 * pair + 128) for m in range(3)]
        for pieces in blocks:
            q, k, v = (
                jnp.concatenate([qkv[piece, col] for piece in pieces], axis=0) for col in cols
            )
            result = attend_pair(q, k, v, bias_ref[pair])
            at = 0
            for piece in pieces:
                size = piece.stop - piece.start
                attended[piece, 128 * pair : 128 * pair + 128] = result[at : at + size]
                at += size


def latitude_kernel(
    member,
    lat_ref,
    x_ref,
    gains_ref,
    qkv_w,
    out_w,
    bias,
    own_ref,
    other_ref,
    state,
    qkv,
    attended,
):
    move = one_hot(
        64,
        128,
        lambda t: t % 8 * 16 + t // 32 * 8 + t // 8 % 2 * 4 + t // 16 % 2 * 2 + member,
    )
    for block in range(8):
        moved = dot(move, x_ref[128 * block : 128 * block + 128])
        for group in range(8):
            start = 64 * group + 8 * block
            state[start : start + 8] = moved[8 * group : 8 * group + 8]
    qkv[...] = dot(normalize(state[...], gains_ref[1:2]), qkv_w[1]).astype(BF)
    attend_blocks(qkv, attended, bias, [[slice(128 * n, 128 * n + 128)] for n in range(4)])
    state[...] = state[...] + dot(attended[...], out_w[1])
    lat = lat_ref[0]
    for pencil in range(4):
        start = pl.multiple_of(128 * pencil + 64 * lat, 64)
        own_ref[pencil] = state[pl.ds(start, 64)]
        start = pl.multiple_of(128 * pencil + 64 * (1 - lat), 64)
        other_ref[pencil] = state[pl.ds(start, 64)].astype(BF)


def column_kernel(
    place_ref,
    first_ref,
    second_ref,
    gains_ref,
    qkv_w,
    out_w,
    bias,
    in_w,
    mlp_w,
    *rest,
):
    out_ref, state, qkv, attended = rest[-4:]
    state[0:256] = first_ref[...].reshape(256, D).astype(F32)
    state[256:512] = second_ref[...].reshape(256, D).astype(F32)
    qkv[...] = dot(normalize(state[...], gains_ref[2:3]), qkv_w[2]).astype(BF)
    blocks = []
    for lon in range(2):
        for part in range(2):
            starts = [256 * lon + 64 * lev + 32 * part for lev in range(LEV)]
            blocks.append([slice(s, s + 32) for s in starts])
    attend_blocks(qkv, attended, bias, blocks)
    state[...] = state[...] + dot(attended[...], out_w[2])
    normed = normalize(state[...], gains_ref[3:4])
    total = state[...]
    for n in range(4):
        cols = slice(FF // 4 * n, FF // 4 * (n + 1))
        u = dot(normed, in_w[:, cols])
        bend = u * (math.sqrt(2 / math.pi) + (math.sqrt(2 / math.pi) * 0.044715) * (u * u))
        hidden = (0.5 * u * (1.0 + jnp.tanh(bend))).astype(BF)
        total = total + dot(hidden, mlp_w[cols])
    for lon in range(2):
        for lev in range(LEV):
            start = 256 * lon + 64 * lev
            out_ref[:, 0, lon, lev, :] = total[start : start + 64]


IN_VMEM = pl.BlockSpec(memory_space=pltpu.VMEM)
IN_HBM = pl.BlockSpec(memory_space=pltpu.HBM)
ANYWHERE = pl.BlockSpec(memory_space=pl.ANY)
DMA = pltpu.SemaphoreType.DMA


def in_hbm(*arrays):
    return [pltpu.with_memory_space_constraint(x, pltpu.HBM) for x in arrays]


def params(mib):
    return pltpu.CompilerParams(vmem_limit_bytes=mib * MIB)


def scratch(tokens):
    return [
        pltpu.VMEM((D, 3 * D), BF),
        pltpu.VMEM((D, D), BF),
        pltpu.VMEM((tokens, D), F32),
        pltpu.VMEM((tokens, 3 * D), BF),
        pltpu.VMEM((tokens, D), BF),
    ]


def pack(fields):
    return pl.pallas_call(
        pack_kernel,
        in_specs=[IN_HBM],
        out_specs=IN_HBM,
        out_shape=pltpu.HBM((1024, D), BF),
        scratch_shapes=[
            pltpu.VMEM((64, 4, LEV, D), F32),
            pltpu.VMEM((1024, D), BF),
            DMA((8,)),
            DMA((8,)),
        ],
        compiler_params=params(16),
        name="pack",
    )(*in_hbm(fields))


def tables(lon_row, lat_row, lev_row):
    return pl.pallas_call(
        tables_kernel,
        in_specs=[IN_VMEM] * 3,
        out_shape=[
            pltpu.HBM((PAIRS, 512, 256), F32),
            pltpu.HBM((PAIRS, 256, 128), F32),
            pltpu.HBM((PAIRS, 256, 128), F32),
        ],
        compiler_params=params(16),
        name="tables",
    )(lon_row, lat_row, lev_row)


def longitude(x, gains, qkv_w, out_w, bias):
    return pl.pallas_call(
        longitude_kernel,
        in_specs=[IN_VMEM] * 2 + [ANYWHERE] * 3,
        out_specs=IN_HBM,
        out_shape=pltpu.HBM((1024, D), BF),
        scratch_shapes=[
            pltpu.VMEM((1024, D), BF),
            pltpu.VMEM((PAIRS, 512, 256), F32),
            *scratch(1024),
            DMA((PAIRS,)),
            DMA((4,)),
            DMA((16,)),
        ],
        compiler_params=params(24),
        name="longitude",
    )(x, gains, *in_hbm(qkv_w, out_w, bias))


def latitude(member, lat, x, gains, qkv_w, out_w, bias):
    return pl.pallas_call(
        lambda *refs: latitude_kernel(member, *refs),
        in_specs=[pl.BlockSpec(memory_space=pltpu.SMEM)] + [IN_VMEM] * 5,
        out_specs=[IN_VMEM, IN_VMEM],
        out_shape=[
            jax.ShapeDtypeStruct((4, 64, D), F32),
            jax.ShapeDtypeStruct((4, 64, D), BF),
        ],
        scratch_shapes=[
            pltpu.VMEM((512, D), F32),
            pltpu.VMEM((512, 3 * D), BF),
            pltpu.VMEM((512, D), BF),
        ],
        compiler_params=params(16),
        name="latitude",
    )(lat, x, gains, qkv_w, out_w, bias)


def column(place, first, second, gains, qkv_w, out_w, bias, mlp_in, mlp_out, out=None):
    in_specs = [IN_VMEM] * 8
    operands = [place, first, second, gains, qkv_w, out_w, bias, mlp_in, mlp_out]
    aliases = {}
    if out is not None:
        in_specs.append(ANYWHERE)
        operands.append(out)
        aliases = {len(operands) - 1: 0}
    return pl.pallas_call(
        column_kernel,
        grid_spec=pltpu.PrefetchScalarGridSpec(
            num_scalar_prefetch=1,
            grid=(1,),
            in_specs=in_specs,
            out_specs=pl.BlockSpec(
                (64, 1, 2, LEV, D),
                lambda _, place_ref: (0, place_ref[0], 0, 0, 0),
                pipeline_mode=pl.Buffered(1),
            ),
            scratch_shapes=[
                pltpu.VMEM((512, D), F32),
                pltpu.VMEM((512, 3 * D), BF),
                pltpu.VMEM((512, D), BF),
            ],
        ),
        out_shape=jax.ShapeDtypeStruct((64, 2, 2, LEV, D), F32),
        input_output_aliases=aliases,
        compiler_params=params(20),
        name="column",
    )(*operands)


def per_device(
    fields,
    norm_gains,
    qkv_weight,
    out_weight,
    longitude_bias,
    latitude_bias,
    level_bias,
    mlp_in,
    mlp_out,
):
    axes = ("lat", "lon")
    spot = lax.axis_index("lat").astype(jnp.int32).reshape(1)
    fields, spot, other_spot = lax.optimization_barrier((fields, spot, 1 - spot))
    latitude_row = jnp.concatenate(
        [latitude_bias[:, 127:], jnp.zeros((HEADS, 1), F32), latitude_bias[:, :127]], axis=1
    )
    offsets = jnp.concatenate([level_bias[:, 3:], jnp.zeros((HEADS, 1), F32), level_bias[:, :3]], axis=1)
    level_row = jnp.concatenate(
        [offsets[:, :, None], jnp.full((HEADS, 8, 31), OUTSIDE, F32)], axis=2
    ).reshape(HEADS, 256)

    def exchange(x):
        return lax.all_to_all(
            x.reshape(128, 8, D), axes, split_axis=0, concat_axis=0, tiled=True
        ).reshape(1024, D)

    circles = exchange(pack(fields))
    lon_table, lat_table, lev_table = tables(longitude_bias, latitude_row, level_row)
    after_circles = longitude(circles, norm_gains, qkv_weight, out_weight, lon_table)
    meridians = exchange(after_circles)
    own, other = [], []
    for member in range(2):
        kept, sent = latitude(member, spot, meridians, norm_gains, qkv_weight, out_weight, lat_table)
        own.append(kept)
        other.append(lax.ppermute(sent, "lat", [(0, 1), (1, 0)]))
    rest = (norm_gains, qkv_weight, out_weight, lev_table, mlp_in, mlp_out)
    out = column(spot, *own, *rest)
    out = column(other_spot, *other, *rest, out=out)
    return out.reshape(64, 4, LEV, D)


def solution(mesh):
    in_specs = (P("lat", "lon", None, None), P(), P(), P(), P(), P(), P(), P(), P())
    out_specs = P("lat", "lon", None, None)
    return jax.shard_map(
        per_device, mesh=mesh, in_specs=in_specs, out_specs=out_specs, check_vma=False
    )
```

```python
import math

import jax
import jax.numpy as jnp
from jax import lax
from jax.experimental import pallas as pl
from jax.experimental.pallas import tpu as pltpu
from jax.sharding import PartitionSpec as P

D = 768
HALF = D // 2
HEADS = 12
PAIRS = HEADS // 2
FF = 3072
LEV = 4
EPS = 1e-06
LOG2E = math.log2(math.e)
SCALE = 0.125 * LOG2E
OUTSIDE = -1e30
MIB = 1 << 20
BF = jnp.bfloat16
F32 = jnp.float32


def dot(a, b):
    return lax.dot_general(a, b, (((1,), (0,)), ((), ())), preferred_element_type=F32)


def dot_t(a, b):
    return lax.dot_general(a, b, (((1,), (1,)), ((), ())), preferred_element_type=F32)


def one_hot(rows, cols, target):
    row = lax.broadcasted_iota(jnp.int32, (rows, cols), 0)
    col = lax.broadcasted_iota(jnp.int32, (rows, cols), 1)
    return jnp.where(target(row) == col, 1.0, 0.0).astype(F32).astype(BF)


def normalize(x, gain):
    square = jnp.mean(x * x, axis=-1, keepdims=True)
    return (x * lax.rsqrt(square + EPS) * gain).astype(BF)


def head_masks():
    lane = lax.broadcasted_iota(jnp.int32, (1, 128), 1)
    even = jnp.where(lane < 64, 1.0, 0.0)
    return even.astype(BF), (1.0 - even).astype(BF)


def toeplitz(row, count, shift=0):
    wide = jnp.broadcast_to(row, (count, 256))
    return pltpu.roll(wide, shift, 1, stride=1, stride_axis=0)


def attend_pair(q, k, v, bias):
    even, odd = head_masks()
    rows, count = q.shape[0], k.shape[0]
    scores = dot_t(jnp.concatenate([q * even, q * odd], axis=0), k) * SCALE + bias
    top = jnp.max(scores, axis=-1, keepdims=True)
    weights = jnp.exp2(scores - top).astype(BF)
    ones = [jnp.broadcast_to(mask, (count, 128)) for mask in (even, odd)]
    values = jnp.concatenate(
        [
            jnp.concatenate([v * even, ones[0]], axis=1),
            jnp.concatenate([v * odd, ones[1]], axis=1),
        ],
        axis=0,
    )
    total = dot(jnp.concatenate([weights[:rows], weights[rows:]], axis=1), values)
    return (total[:, :128] / total[:, 128:]).astype(BF)


def fetch(source, target, sem):
    copy = pltpu.make_async_copy(source, target, sem)
    copy.start()
    return copy


def pack_kernel(
    fields_ref, lon_ref, lat_ref, lev_ref, out_ref, lon_out, lat_out, lev_out, x, sems
):
    loads = [
        fetch(fields_ref.at[pl.ds(8 * n, 8)], x.at[pl.ds(8 * n, 8)], sems.at[n]) for n in range(8)
    ]
    lon = lon_ref[...] * LOG2E
    lat = jnp.concatenate([lat_ref[...], jnp.zeros((HEADS, 1), F32)], axis=1) * LOG2E
    lane = lax.broadcasted_iota(jnp.int32, (HEADS, 256), 1)
    lev = jnp.full((HEADS, 256), OUTSIDE, F32)
    for step in range(1 - LEV, LEV):
        lev = jnp.where(lane == 32 * step % 256, lev_ref[:, step + LEV - 1 : step + LEV] * LOG2E, lev)
    for head in range(HEADS):
        pair, row = head // 2, slice(head, head + 1)
        rows = 256 * (head % 2)
        lon_out[pair, rows : rows + 256] = toeplitz(lon[row], 256)
        rows = 128 * (head % 2)
        lat_out[pair, rows : rows + 128] = toeplitz(lat[row], 128, 129)[:, :128]
        lev_out[pair, rows : rows + 128] = toeplitz(lev[row], 128)[:, :128]
    move = one_hot(128, 128, lambda r: r // 16 * 16 + r % 4 * 4 + r // 4 % 4)
    for n in range(8):
        loads[n].wait()
        rows = slice(128 * n, 128 * n + 128)
        out_ref[rows] = dot(move, x[8 * n : 8 * n + 8].reshape(128, D).astype(BF)).astype(BF)


def longitude_kernel(
    x_ref, gains_ref, qkv_w_hbm, out_w, bias, out_ref, qkv_w, x, state, qkv, attended, sems
):
    parts = [pl.ds(D * n, D) for n in range(3)]
    loads = [
        fetch(qkv_w_hbm.at[0, :, part], qkv_w.at[:, part], sems.at[n])
        for n, part in enumerate(parts)
    ]
    move = one_hot(128, 128, lambda t: t % 64 // 4 * 8 + t // 64 * 4 + t % 4)
    for block in range(8):
        moved = dot(move, x_ref[128 * block : 128 * block + 128])
        for level in range(2):
            start = 512 * (block // 4) + 256 * level + 64 * (block % 4)
            state[start : start + 64] = moved[64 * level : 64 * level + 64]
    normed = normalize(state[...], gains_ref[0:1])
    for load, part in zip(loads, parts):
        load.wait()
        qkv[:, part] = dot(normed, qkv_w[:, part]).astype(BF)
    attend_blocks(qkv, attended, bias, [[slice(256 * n, 256 * n + 256)] for n in range(4)])
    x[...] = (state[...] + dot(attended[...], out_w[0])).astype(BF)
    move = one_hot(
        128,
        128,
        lambda r: r // 2 % 4 * 32 + r // 8 % 8 * 4 + r // 64 * 2 + r % 2,
    )
    for block in range(8):
        tokens = jnp.concatenate(
            [x[256 * n + 32 * block : 256 * n + 32 * block + 32] for n in range(4)], axis=0
        )
        moved = dot(move, tokens).astype(BF)
        for lat in range(2):
            start = 512 * lat + 64 * block
            out_ref[start : start + 64] = moved[64 * lat : 64 * lat + 64]


def attend_blocks(qkv, attended, bias, blocks):
    def attend_heads(pair, _):
        cols = [pl.ds(pl.multiple_of(m * D + 128 * pair, 128), 128) for m in range(3)]
        table = bias[pair]
        for pieces in blocks:
            q, k, v = (
                jnp.concatenate([qkv[piece, col] for piece in pieces], axis=0) for col in cols
            )
            result = attend_pair(q, k, v, table)
            at = 0
            for piece in pieces:
                size = piece.stop - piece.start
                attended[piece, cols[0]] = result[at : at + size]
                at += size
        return 0

    lax.fori_loop(0, PAIRS, attend_heads, 0, unroll=True)


def latitude_kernel(
    member,
    lat_ref,
    x_ref,
    gains_ref,
    qkv_w,
    out_w,
    bias,
    own_ref,
    other_ref,
    state,
    qkv,
    attended,
):
    move = one_hot(
        64,
        128,
        lambda t: t % 8 * 16 + t // 32 * 8 + t // 8 % 2 * 4 + t // 16 % 2 * 2 + member,
    )
    for block in range(8):
        moved = dot(move, x_ref[128 * block : 128 * block + 128])
        for group in range(8):
            start = 64 * group + 8 * block
            state[start : start + 8] = moved[8 * group : 8 * group + 8]
    qkv[...] = dot(normalize(state[...], gains_ref[1:2]), qkv_w[1]).astype(BF)
    attend_blocks(qkv, attended, bias, [[slice(128 * n, 128 * n + 128)] for n in range(4)])
    state[...] = state[...] + dot(attended[...], out_w[1])
    lat = lat_ref[0]
    for pencil in range(4):
        start = pl.multiple_of(128 * pencil + 64 * lat, 64)
        own_ref[pencil] = state[pl.ds(start, 64)]
        start = pl.multiple_of(128 * pencil + 64 * (1 - lat), 64)
        other_ref[pencil] = state[pl.ds(start, 64)].astype(BF)


def column_kernel(
    place_ref,
    first_ref,
    second_ref,
    gains_ref,
    qkv_w,
    out_w,
    bias,
    in_w,
    mlp_w,
    *rest,
):
    out_ref, state, qkv, attended = rest[-4:]
    state[0:256] = first_ref[...].reshape(256, D).astype(F32)
    state[256:512] = second_ref[...].reshape(256, D).astype(F32)
    qkv[...] = dot(normalize(state[...], gains_ref[2:3]), qkv_w[2]).astype(BF)
    blocks = []
    for lon in range(2):
        for part in range(2):
            starts = [256 * lon + 64 * lev + 32 * part for lev in range(LEV)]
            blocks.append([slice(s, s + 32) for s in starts])
    attend_blocks(qkv, attended, bias, blocks)
    state[...] = state[...] + dot(attended[...], out_w[2])
    normed = normalize(state[...], gains_ref[3:4])
    total = state[...]
    for n in range(4):
        cols = slice(FF // 4 * n, FF // 4 * (n + 1))
        u = dot(normed, in_w[:, cols])
        bend = u * (math.sqrt(2 / math.pi) + (math.sqrt(2 / math.pi) * 0.044715) * (u * u))
        hidden = (0.5 * u * (1.0 + jnp.tanh(bend))).astype(BF)
        total = total + dot(hidden, mlp_w[cols])
    for lon in range(2):
        for lev in range(LEV):
            start = 256 * lon + 64 * lev
            out_ref[:, 0, lon, lev, :] = total[start : start + 64]


IN_VMEM = pl.BlockSpec(memory_space=pltpu.VMEM)
IN_HBM = pl.BlockSpec(memory_space=pltpu.HBM)
ANYWHERE = pl.BlockSpec(memory_space=pl.ANY)
DMA = pltpu.SemaphoreType.DMA


def in_hbm(*arrays):
    return [pltpu.with_memory_space_constraint(x, pltpu.HBM) for x in arrays]


def params(mib):
    return pltpu.CompilerParams(vmem_limit_bytes=mib * MIB)


def scratch(tokens):
    return [
        pltpu.VMEM((tokens, D), F32),
        pltpu.VMEM((tokens, 3 * D), BF),
        pltpu.VMEM((tokens, D), BF),
    ]


def pack(fields, lon_bias, lat_bias, lev_bias):
    return pl.pallas_call(
        pack_kernel,
        in_specs=[IN_HBM] + [IN_VMEM] * 3,
        out_specs=[IN_VMEM] * 4,
        out_shape=[
            pltpu.VMEM((1024, D), BF),
            pltpu.VMEM((PAIRS, 512, 256), F32),
            pltpu.VMEM((PAIRS, 256, 128), F32),
            pltpu.VMEM((PAIRS, 256, 128), F32),
        ],
        scratch_shapes=[pltpu.VMEM((64, 4, LEV, D), F32), DMA((8,))],
        compiler_params=params(12),
        name="pack",
    )(*in_hbm(fields), lon_bias, lat_bias, lev_bias)


def longitude(x, gains, qkv_w, out_w, bias):
    return pl.pallas_call(
        longitude_kernel,
        in_specs=[IN_VMEM] * 2 + [ANYWHERE] + [IN_VMEM] * 2,
        out_specs=IN_VMEM,
        out_shape=pltpu.VMEM((1024, D), BF),
        scratch_shapes=[
            pltpu.VMEM((D, 3 * D), BF),
            pltpu.VMEM((1024, D), BF),
            *scratch(1024),
            DMA((3,)),
        ],
        compiler_params=params(24),
        name="longitude",
    )(x, gains, *in_hbm(qkv_w), out_w, bias)


def latitude(member, lat, x, gains, qkv_w, out_w, bias):
    return pl.pallas_call(
        lambda *refs: latitude_kernel(member, *refs),
        in_specs=[pl.BlockSpec(memory_space=pltpu.SMEM)] + [IN_VMEM] * 5,
        out_specs=[IN_VMEM, IN_VMEM],
        out_shape=[
            jax.ShapeDtypeStruct((4, 64, D), F32),
            jax.ShapeDtypeStruct((4, 64, D), BF),
        ],
        scratch_shapes=[
            *scratch(512),
        ],
        compiler_params=params(16),
        name="latitude",
    )(lat, x, gains, qkv_w, out_w, bias)


def column(place, first, second, gains, qkv_w, out_w, bias, mlp_in, mlp_out, out=None):
    in_specs = [IN_VMEM] * 8
    operands = [place, first, second, gains, qkv_w, out_w, bias, mlp_in, mlp_out]
    aliases = {}
    if out is not None:
        in_specs.append(ANYWHERE)
        operands.append(out)
        aliases = {len(operands) - 1: 0}
    return pl.pallas_call(
        column_kernel,
        grid_spec=pltpu.PrefetchScalarGridSpec(
            num_scalar_prefetch=1,
            grid=(1,),
            in_specs=in_specs,
            out_specs=pl.BlockSpec(
                (64, 1, 2, LEV, D),
                lambda _, place_ref: (0, place_ref[0], 0, 0, 0),
                pipeline_mode=pl.Buffered(1),
            ),
            scratch_shapes=[
                pltpu.VMEM((512, D), F32),
                pltpu.VMEM((512, 3 * D), BF),
                pltpu.VMEM((512, D), BF),
            ],
        ),
        out_shape=jax.ShapeDtypeStruct((64, 2, 2, LEV, D), F32),
        input_output_aliases=aliases,
        compiler_params=params(20),
        name="column",
    )(*operands)


def per_device(
    fields,
    norm_gains,
    qkv_weight,
    out_weight,
    longitude_bias,
    latitude_bias,
    level_bias,
    mlp_in,
    mlp_out,
):
    axes = ("lat", "lon")
    spot = lax.axis_index("lat").astype(jnp.int32).reshape(1)
    fields, spot, other_spot = lax.optimization_barrier((fields, spot, 1 - spot))
    def exchange(x):
        return lax.all_to_all(
            x.reshape(128, 8, D), axes, split_axis=0, concat_axis=0, tiled=True
        ).reshape(1024, D)

    packed, lon_table, lat_table, lev_table = pack(
        fields, longitude_bias, latitude_bias, level_bias
    )
    circles = exchange(packed)
    after_circles = longitude(circles, norm_gains, qkv_weight, out_weight, lon_table)
    meridians = exchange(after_circles)
    own, other = [], []
    for member in range(2):
        kept, sent = latitude(member, spot, meridians, norm_gains, qkv_weight, out_weight, lat_table)
        own.append(kept)
        other.append(lax.ppermute(sent, "lat", [(0, 1), (1, 0)]))
    rest = (norm_gains, qkv_weight, out_weight, lev_table, mlp_in, mlp_out)
    out = column(spot, *own, *rest)
    out = column(other_spot, *other, *rest, out=out)
    return out.reshape(64, 4, LEV, D)


def solution(mesh):
    in_specs = (P("lat", "lon", None, None), P(), P(), P(), P(), P(), P(), P(), P())
    out_specs = P("lat", "lon", None, None)
    return jax.shard_map(
        per_device, mesh=mesh, in_specs=in_specs, out_specs=out_specs, check_vma=False
    )
```

```python
import math

import jax
import jax.numpy as jnp
from jax import lax
from jax.experimental import pallas as pl
from jax.experimental.pallas import tpu as pltpu
from jax.sharding import PartitionSpec as P

D = 768
HALF = D // 2
HEADS = 12
PAIRS = HEADS // 2
FF = 3072
LEV = 4
EPS = 1e-06
LOG2E = math.log2(math.e)
SCALE = 0.125 * LOG2E
OUTSIDE = -1e30
MIB = 1 << 20
BF = jnp.bfloat16
F32 = jnp.float32


def dot(a, b):
    return lax.dot_general(a, b, (((1,), (0,)), ((), ())), preferred_element_type=F32)


def dot_t(a, b):
    return lax.dot_general(a, b, (((1,), (1,)), ((), ())), preferred_element_type=F32)


def one_hot(rows, cols, target):
    row = lax.broadcasted_iota(jnp.int32, (rows, cols), 0)
    col = lax.broadcasted_iota(jnp.int32, (rows, cols), 1)
    return jnp.where(target(row) == col, 1.0, 0.0).astype(F32).astype(BF)


def normalize(x, gain):
    square = jnp.mean(x * x, axis=-1, keepdims=True)
    return (x * lax.rsqrt(square + EPS) * gain).astype(BF)


def head_masks():
    lane = lax.broadcasted_iota(jnp.int32, (1, 128), 1)
    even = jnp.where(lane < 64, 1.0, 0.0)
    return even.astype(BF), (1.0 - even).astype(BF)


def toeplitz(row, count, shift=0):
    wide = jnp.broadcast_to(row, (count, 256))
    return pltpu.roll(wide, shift, 1, stride=1, stride_axis=0)


def attend_pair(q, k, v, bias):
    even, odd = head_masks()
    rows, count = q.shape[0], k.shape[0]
    scores = dot_t(jnp.concatenate([q * even, q * odd], axis=0), k) * SCALE + bias
    top = jnp.max(scores, axis=-1, keepdims=True)
    weights = jnp.exp2(scores - top).astype(BF)
    ones = [jnp.broadcast_to(mask, (count, 128)) for mask in (even, odd)]
    values = jnp.concatenate(
        [
            jnp.concatenate([v * even, ones[0]], axis=1),
            jnp.concatenate([v * odd, ones[1]], axis=1),
        ],
        axis=0,
    )
    total = dot(jnp.concatenate([weights[:rows], weights[rows:]], axis=1), values)
    return (total[:, :128] / total[:, 128:]).astype(BF)


def fetch(source, target, sem):
    copy = pltpu.make_async_copy(source, target, sem)
    copy.start()
    return copy


def pack_kernel(
    fields_ref,
    lon_ref,
    lat_ref,
    lev_ref,
    out_ref,
    lon_out,
    lat_out,
    lev_out,
    x,
    lon,
    lat,
    lev,
    sems,
    bias_sems,
):
    biases = [
        fetch(source, target, bias_sems.at[n])
        for n, (source, target) in enumerate(((lon_ref, lon), (lat_ref, lat), (lev_ref, lev)))
    ]
    loads = [
        fetch(fields_ref.at[pl.ds(8 * n, 8)], x.at[pl.ds(8 * n, 8)], sems.at[n]) for n in range(8)
    ]
    for bias in biases:
        bias.wait()
    lon_rows = lon[...] * LOG2E
    lat_rows = jnp.concatenate([lat[...], jnp.zeros((HEADS, 1), F32)], axis=1) * LOG2E
    lane = lax.broadcasted_iota(jnp.int32, (1, 256), 1)
    for head in range(HEADS):
        pair, row = head // 2, slice(head, head + 1)
        lev_row = jnp.full((1, 256), OUTSIDE, F32)
        for step in range(1 - LEV, LEV):
            value = lev[step + LEV - 1 : step + LEV, row] * LOG2E
            lev_row = jnp.where(lane == 32 * step % 256, value, lev_row)
        rows = 256 * (head % 2)
        lon_out[pair, rows : rows + 256] = toeplitz(lon_rows[row], 256)
        rows = 128 * (head % 2)
        lat_out[pair, rows : rows + 128] = toeplitz(lat_rows[row], 128, 129)[:, :128]
        lev_out[pair, rows : rows + 128] = toeplitz(lev_row, 128)[:, :128]
    move = one_hot(128, 128, lambda r: r // 16 * 16 + r % 4 * 4 + r // 4 % 4)
    for n in range(8):
        loads[n].wait()
        rows = slice(128 * n, 128 * n + 128)
        out_ref[rows] = dot(move, x[8 * n : 8 * n + 8].reshape(128, D).astype(BF)).astype(BF)


def longitude_kernel(
    x_ref, gains_ref, qkv_w_hbm, out_w, bias, out_ref, qkv_w, x, state, qkv, attended, sems
):
    parts = [pl.ds(D * n, D) for n in range(3)]
    loads = [
        fetch(qkv_w_hbm.at[0, :, part], qkv_w.at[:, part], sems.at[n])
        for n, part in enumerate(parts)
    ]
    move = one_hot(128, 128, lambda t: t % 64 // 4 * 8 + t // 64 * 4 + t % 4)
    for block in range(8):
        moved = dot(move, x_ref[128 * block : 128 * block + 128])
        for level in range(2):
            start = 512 * (block // 4) + 256 * level + 64 * (block % 4)
            state[start : start + 64] = moved[64 * level : 64 * level + 64]
    normed = normalize(state[...], gains_ref[0:1])
    for load, part in zip(loads, parts):
        load.wait()
        qkv[:, part] = dot(normed, qkv_w[:, part]).astype(BF)
    attend_blocks(qkv, attended, bias, [[slice(256 * n, 256 * n + 256)] for n in range(4)])
    x[...] = (state[...] + dot(attended[...], out_w[0])).astype(BF)
    move = one_hot(
        128,
        128,
        lambda r: r // 2 % 4 * 32 + r // 8 % 8 * 4 + r // 64 * 2 + r % 2,
    )
    for block in range(8):
        tokens = jnp.concatenate(
            [x[256 * n + 32 * block : 256 * n + 32 * block + 32] for n in range(4)], axis=0
        )
        moved = dot(move, tokens).astype(BF)
        for lat in range(2):
            start = 512 * lat + 64 * block
            out_ref[start : start + 64] = moved[64 * lat : 64 * lat + 64]


def attend_blocks(qkv, attended, bias, blocks):
    def attend_heads(pair, _):
        cols = [pl.ds(pl.multiple_of(m * D + 128 * pair, 128), 128) for m in range(3)]
        table = bias[pair]
        for pieces in blocks:
            q, k, v = (
                jnp.concatenate([qkv[piece, col] for piece in pieces], axis=0) for col in cols
            )
            result = attend_pair(q, k, v, table)
            at = 0
            for piece in pieces:
                size = piece.stop - piece.start
                attended[piece, cols[0]] = result[at : at + size]
                at += size
        return 0

    lax.fori_loop(0, PAIRS, attend_heads, 0, unroll=True)


def latitude_kernel(
    member,
    lat_ref,
    x_ref,
    gains_ref,
    qkv_w,
    out_w,
    bias,
    own_low,
    own_high,
    other_low,
    other_high,
    state,
    qkv,
    attended,
):
    move = one_hot(
        64,
        128,
        lambda t: t % 8 * 16 + t // 32 * 8 + t // 8 % 2 * 4 + t // 16 % 2 * 2 + member,
    )
    for block in range(8):
        moved = dot(move, x_ref[128 * block : 128 * block + 128])
        for group in range(8):
            start = 64 * group + 8 * block
            state[start : start + 8] = moved[8 * group : 8 * group + 8]
    qkv[...] = dot(normalize(state[...], gains_ref[1:2]), qkv_w[1]).astype(BF)
    attend_blocks(qkv, attended, bias, [[slice(128 * n, 128 * n + 128)] for n in range(4)])
    state[...] = state[...] + dot(attended[...], out_w[1])
    lat = lat_ref[0]
    for lev in range(LEV):
        start = pl.multiple_of(128 * lev + 64 * lat, 64)
        (own_low, own_high)[lev // 2][lev % 2] = state[pl.ds(start, 64)]
        start = pl.multiple_of(128 * lev + 64 * (1 - lat), 64)
        (other_low, other_high)[lev // 2][lev % 2] = state[pl.ds(start, 64)].astype(BF)


def column_kernel(place_ref, *refs):
    pieces, (gains_ref, qkv_w, out_w, bias, in_w, mlp_w) = refs[:4], refs[4:10]
    out_hbm, state, qkv, attended, result, sems = refs[-6:]
    for n, piece in enumerate(pieces):
        state[128 * n : 128 * n + 128] = piece[...].reshape(128, D).astype(F32)
    qkv[...] = dot(normalize(state[...], gains_ref[2:3]), qkv_w[2]).astype(BF)
    blocks = []
    for lon in range(2):
        for part in range(2):
            starts = [256 * lon + 64 * lev + 32 * part for lev in range(LEV)]
            blocks.append([slice(s, s + 32) for s in starts])
    attend_blocks(qkv, attended, bias, blocks)
    state[...] = state[...] + dot(attended[...], out_w[2])
    normed = normalize(state[...], gains_ref[3:4])
    total = state[...]
    for n in range(4):
        cols = slice(FF // 4 * n, FF // 4 * (n + 1))
        u = dot(normed, in_w[:, cols])
        bend = u * (math.sqrt(2 / math.pi) + (math.sqrt(2 / math.pi) * 0.044715) * (u * u))
        hidden = (0.5 * u * (1.0 + jnp.tanh(bend))).astype(BF)
        if n < 3:
            total = total + dot(hidden, mlp_w[cols])
    stores = []
    for lon in range(2):
        rows = slice(256 * lon, 256 * lon + 256)
        final = total[rows] + dot(hidden[rows], mlp_w[cols])
        for lev in range(LEV):
            result[lon, :, lev, :] = final[64 * lev : 64 * lev + 64]
        stores.append(fetch(result.at[lon], out_hbm.at[:, place_ref[0], lon], sems.at[lon]))
    for store in stores:
        store.wait()


IN_VMEM = pl.BlockSpec(memory_space=pltpu.VMEM)
IN_HBM = pl.BlockSpec(memory_space=pltpu.HBM)
ANYWHERE = pl.BlockSpec(memory_space=pl.ANY)
DMA = pltpu.SemaphoreType.DMA


def in_hbm(*arrays):
    return [pltpu.with_memory_space_constraint(x, pltpu.HBM) for x in arrays]


def params(mib):
    return pltpu.CompilerParams(vmem_limit_bytes=mib * MIB)


def scratch(tokens):
    return [
        pltpu.VMEM((tokens, D), F32),
        pltpu.VMEM((tokens, 3 * D), BF),
        pltpu.VMEM((tokens, D), BF),
    ]


def pack(fields, lon_bias, lat_bias, lev_bias):
    return pl.pallas_call(
        pack_kernel,
        in_specs=[ANYWHERE] * 4,
        out_specs=[IN_VMEM] * 4,
        out_shape=[
            pltpu.VMEM((1024, D), BF),
            pltpu.VMEM((PAIRS, 512, 256), F32),
            pltpu.VMEM((PAIRS, 256, 128), F32),
            pltpu.VMEM((PAIRS, 256, 128), F32),
        ],
        scratch_shapes=[
            pltpu.VMEM((64, 4, LEV, D), F32),
            pltpu.VMEM((HEADS, 256), F32),
            pltpu.VMEM((HEADS, 255), F32),
            pltpu.VMEM((7, HEADS), F32),
            DMA((8,)),
            DMA((3,)),
        ],
        compiler_params=params(12),
        name="pack",
    )(*in_hbm(fields, lon_bias, lat_bias, lev_bias.T))


def longitude(x, gains, qkv_w, out_w, bias):
    return pl.pallas_call(
        longitude_kernel,
        in_specs=[IN_VMEM] * 2 + [ANYWHERE] + [IN_VMEM] * 2,
        out_specs=IN_VMEM,
        out_shape=pltpu.VMEM((1024, D), BF),
        scratch_shapes=[
            pltpu.VMEM((D, 3 * D), BF),
            pltpu.VMEM((1024, D), BF),
            *scratch(1024),
            DMA((3,)),
        ],
        compiler_params=params(24),
        name="longitude",
    )(x, gains, *in_hbm(qkv_w), out_w, bias)


def latitude(member, lat, x, gains, qkv_w, out_w, bias):
    return pl.pallas_call(
        lambda *refs: latitude_kernel(member, *refs),
        in_specs=[pl.BlockSpec(memory_space=pltpu.SMEM)] + [IN_VMEM] * 5,
        out_specs=[IN_VMEM] * 4,
        out_shape=[pltpu.VMEM((2, 64, D), F32)] * 2 + [pltpu.VMEM((2, 64, D), BF)] * 2,
        scratch_shapes=[
            *scratch(512),
        ],
        compiler_params=params(16),
        name="latitude",
    )(lat, x, gains, qkv_w, out_w, bias)


def column(place, pieces, gains, qkv_w, out_w, bias, mlp_in, mlp_out, out=None):
    in_specs = [pl.BlockSpec(memory_space=pltpu.SMEM)] + [IN_VMEM] * 10
    operands = [place, *pieces, gains, qkv_w, out_w, bias, mlp_in, mlp_out]
    aliases = {}
    if out is not None:
        in_specs.append(ANYWHERE)
        operands.append(out)
        aliases = {len(operands) - 1: 0}
    return pl.pallas_call(
        column_kernel,
        in_specs=in_specs,
        out_specs=IN_HBM,
        out_shape=pltpu.HBM((64, 2, 2, LEV, D), F32),
        scratch_shapes=[*scratch(512), pltpu.VMEM((2, 64, LEV, D), F32), DMA((2,))],
        input_output_aliases=aliases,
        compiler_params=params(20),
        name="column",
    )(*operands)


def per_device(
    fields,
    norm_gains,
    qkv_weight,
    out_weight,
    longitude_bias,
    latitude_bias,
    level_bias,
    mlp_in,
    mlp_out,
):
    axes = ("lat", "lon")
    spot = lax.axis_index("lat").astype(jnp.int32).reshape(1)
    fields, spot, other_spot = lax.optimization_barrier((fields, spot, 1 - spot))
    def exchange(x):
        return lax.all_to_all(
            x.reshape(128, 8, D), axes, split_axis=0, concat_axis=0, tiled=True
        ).reshape(1024, D)

    packed, lon_table, lat_table, lev_table = pack(
        fields, longitude_bias, latitude_bias, level_bias
    )
    circles = exchange(packed)
    after_circles = longitude(circles, norm_gains, qkv_weight, out_weight, lon_table)
    meridians = exchange(after_circles)
    own, sent = [], []
    for member in range(2):
        made = latitude(member, spot, meridians, norm_gains, qkv_weight, out_weight, lat_table)
        own += made[:2]
        sent += made[2:]

    def swap(x):
        return lax.ppermute(x, "lat", [(0, 1), (1, 0)])

    held = lax.optimization_barrier((swap(sent[0]), *sent[1:]))
    other = [held[0], *(swap(x) for x in held[1:])]
    rest = (norm_gains, qkv_weight, out_weight, lev_table, mlp_in, mlp_out)
    out = column(spot, own, *rest)
    out = column(other_spot, other, *rest, out=out)
    return out.reshape(64, 4, LEV, D)


def solution(mesh):
    in_specs = (P("lat", "lon", None, None), P(), P(), P(), P(), P(), P(), P(), P())
    out_specs = P("lat", "lon", None, None)
    return jax.shard_map(
        per_device, mesh=mesh, in_specs=in_specs, out_specs=out_specs, check_vma=False
    )
```

```python
import math

import jax
import jax.numpy as jnp
from jax import lax
from jax.experimental import pallas as pl
from jax.experimental.pallas import tpu as pltpu
from jax.sharding import PartitionSpec as P

D = 768
HALF = D // 2
HEADS = 12
PAIRS = HEADS // 2
FF = 3072
LEV = 4
EPS = 1e-06
LOG2E = math.log2(math.e)
SCALE = 0.125 * LOG2E
OUTSIDE = -1e30
MIB = 1 << 20
BF = jnp.bfloat16
F32 = jnp.float32


def dot(a, b):
    return lax.dot_general(a, b, (((1,), (0,)), ((), ())), preferred_element_type=F32)


def dot_t(a, b):
    return lax.dot_general(a, b, (((1,), (1,)), ((), ())), preferred_element_type=F32)


def one_hot(rows, cols, target):
    row = lax.broadcasted_iota(jnp.int32, (rows, cols), 0)
    col = lax.broadcasted_iota(jnp.int32, (rows, cols), 1)
    return jnp.where(target(row) == col, 1.0, 0.0).astype(F32).astype(BF)


def normalize(x, gain):
    square = jnp.mean(x * x, axis=-1, keepdims=True)
    return (x * lax.rsqrt(square + EPS) * gain).astype(BF)


def head_masks():
    lane = lax.broadcasted_iota(jnp.int32, (1, 128), 1)
    even = jnp.where(lane < 64, 1.0, 0.0)
    return even.astype(BF), (1.0 - even).astype(BF)


def toeplitz(row, count, shift=0):
    wide = jnp.broadcast_to(row, (count, 256))
    return pltpu.roll(wide, shift, 1, stride=1, stride_axis=0)


def attend_pair(q, k, v, bias):
    even, odd = head_masks()
    rows, count = q.shape[0], k.shape[0]
    scores = dot_t(jnp.concatenate([q * even, q * odd], axis=0), k) * SCALE + bias
    top = jnp.max(scores, axis=-1, keepdims=True)
    weights = jnp.exp2(scores - top).astype(BF)
    ones = [jnp.broadcast_to(mask, (count, 128)) for mask in (even, odd)]
    values = jnp.concatenate(
        [
            jnp.concatenate([v * even, ones[0]], axis=1),
            jnp.concatenate([v * odd, ones[1]], axis=1),
        ],
        axis=0,
    )
    total = dot(jnp.concatenate([weights[:rows], weights[rows:]], axis=1), values)
    return (total[:, :128] / total[:, 128:]).astype(BF)


def fetch(source, target, sem):
    copy = pltpu.make_async_copy(source, target, sem)
    copy.start()
    return copy


def pack_kernel(fields_ref, out_ref, x, sems):
    loads = [
        fetch(fields_ref.at[pl.ds(8 * n, 8)], x.at[pl.ds(8 * n, 8)], sems.at[n]) for n in range(8)
    ]
    move = one_hot(128, 128, lambda r: r // 16 * 16 + r % 4 * 4 + r // 4 % 4)
    for n in range(8):
        loads[n].wait()
        rows = slice(128 * n, 128 * n + 128)
        out_ref[rows] = dot(move, x[8 * n : 8 * n + 8].reshape(128, D).astype(BF)).astype(BF)


def toeplitz_pair(rows, count, shift=0):
    return jnp.concatenate([toeplitz(row, count, shift)[:, :count] for row in rows], axis=0)


def level_rows(lev_ref):
    lane = lax.broadcasted_iota(jnp.int32, (1, 256), 1)
    rows = []
    for head in range(HEADS):
        row = jnp.full((1, 256), OUTSIDE, F32)
        for step in range(1 - LEV, LEV):
            value = lev_ref[step + LEV - 1 : step + LEV, head : head + 1] * LOG2E
            row = jnp.where(lane == 32 * step % 256, value, row)
        rows.append(row)
    return rows


def longitude_kernel(
    x_ref, gains_ref, qkv_w_hbm, out_w, bias_ref, out_ref, qkv_w, x, state, qkv, attended, sems
):
    parts = [pl.ds(D * n, D) for n in range(3)]
    loads = [
        fetch(qkv_w_hbm.at[0, :, part], qkv_w.at[:, part], sems.at[n])
        for n, part in enumerate(parts)
    ]
    move = one_hot(128, 128, lambda t: t % 64 // 4 * 8 + t // 64 * 4 + t % 4)
    for block in range(8):
        moved = dot(move, x_ref[128 * block : 128 * block + 128])
        for level in range(2):
            start = 512 * (block // 4) + 256 * level + 64 * (block % 4)
            state[start : start + 64] = moved[64 * level : 64 * level + 64]
    normed = normalize(state[...], gains_ref[0:1])
    for load, part in zip(loads, parts):
        load.wait()
        qkv[:, part] = dot(normed, qkv_w[:, part]).astype(BF)
    rows = bias_ref[...] * LOG2E
    attend_blocks(
        qkv,
        attended,
        lambda pair: toeplitz_pair([rows[2 * pair + e : 2 * pair + e + 1] for e in range(2)], 256),
        [[slice(256 * n, 256 * n + 256)] for n in range(4)],
    )
    x[...] = (state[...] + dot(attended[...], out_w[0])).astype(BF)
    move = one_hot(
        128,
        128,
        lambda r: r // 2 % 4 * 32 + r // 8 % 8 * 4 + r // 64 * 2 + r % 2,
    )
    for block in range(8):
        tokens = jnp.concatenate(
            [x[256 * n + 32 * block : 256 * n + 32 * block + 32] for n in range(4)], axis=0
        )
        moved = dot(move, tokens).astype(BF)
        for lat in range(2):
            start = 512 * lat + 64 * block
            out_ref[start : start + 64] = moved[64 * lat : 64 * lat + 64]


def attend_blocks(qkv, attended, table_of, blocks):
    for pair in range(PAIRS):
        cols = [slice(m * D + 128 * pair, m * D + 128 * pair + 128) for m in range(3)]
        table = table_of(pair)
        for pieces in blocks:
            q, k, v = (
                jnp.concatenate([qkv[piece, col] for piece in pieces], axis=0) for col in cols
            )
            result = attend_pair(q, k, v, table)
            at = 0
            for piece in pieces:
                size = piece.stop - piece.start
                attended[piece, cols[0]] = result[at : at + size]
                at += size


def latitude_kernel(member, lat_ref, x_ref, gains_ref, qkv_w, out_w, bias_ref, *refs):
    own_ref, *others, state, qkv, attended = refs[member:]
    move = one_hot(
        64,
        128,
        lambda t: t % 8 * 16 + t // 32 * 8 + t // 8 % 2 * 4 + t // 16 % 2 * 2 + member,
    )
    for block in range(8):
        moved = dot(move, x_ref[128 * block : 128 * block + 128])
        for group in range(8):
            start = 64 * group + 8 * block
            state[start : start + 8] = moved[8 * group : 8 * group + 8]
    qkv[...] = dot(normalize(state[...], gains_ref[1:2]), qkv_w[1]).astype(BF)
    rows = jnp.concatenate([bias_ref[...], jnp.zeros((HEADS, 1), F32)], axis=1) * LOG2E
    attend_blocks(
        qkv,
        attended,
        lambda pair: toeplitz_pair(
            [rows[2 * pair + e : 2 * pair + e + 1] for e in range(2)], 128, 129
        ),
        [[slice(128 * n, 128 * n + 128)] for n in range(4)],
    )
    state[...] = state[...] + dot(attended[...], out_w[1])
    lat = lat_ref[0]
    if member:
        others[0][0:2] = refs[0][...]
        targets = [others[0].at[2 + lev] for lev in range(LEV)]
    else:
        targets = [others[lev // 2].at[lev % 2] for lev in range(LEV)]
    for lev in range(LEV):
        start = pl.multiple_of(128 * lev + 64 * lat, 64)
        own_ref[lev] = state[pl.ds(start, 64)]
        start = pl.multiple_of(128 * lev + 64 * (1 - lat), 64)
        targets[lev][...] = state[pl.ds(start, 64)].astype(BF)


def column_kernel(place_ref, *refs):
    pieces, (gains_ref, qkv_w, out_w, bias_ref, in_w, mlp_w) = refs[:2], refs[2:8]
    out_hbm, state, qkv, attended, result, sems = refs[-6:]
    at = 0
    for piece in pieces:
        size = 64 * piece.shape[0]
        state[at : at + size] = piece[...].reshape(size, D).astype(F32)
        at += size
    qkv[...] = dot(normalize(state[...], gains_ref[2:3]), qkv_w[2]).astype(BF)
    blocks = []
    for lon in range(2):
        for part in range(2):
            starts = [256 * lon + 64 * lev + 32 * part for lev in range(LEV)]
            blocks.append([slice(s, s + 32) for s in starts])
    rows = level_rows(bias_ref)
    attend_blocks(
        qkv, attended, lambda pair: toeplitz_pair(rows[2 * pair : 2 * pair + 2], 128), blocks
    )
    state[...] = state[...] + dot(attended[...], out_w[2])
    normed = normalize(state[...], gains_ref[3:4])
    total = state[...]
    for n in range(4):
        cols = slice(FF // 4 * n, FF // 4 * (n + 1))
        u = dot(normed, in_w[:, cols])
        bend = u * (math.sqrt(2 / math.pi) + (math.sqrt(2 / math.pi) * 0.044715) * (u * u))
        hidden = (0.5 * u * (1.0 + jnp.tanh(bend))).astype(BF)
        if n < 3:
            total = total + dot(hidden, mlp_w[cols])
    stores = []
    for lon in range(2):
        rows = slice(256 * lon, 256 * lon + 256)
        final = total[rows] + dot(hidden[rows], mlp_w[cols])
        for lev in range(LEV):
            result[lon, :, lev, :] = final[64 * lev : 64 * lev + 64]
        stores.append(fetch(result.at[lon], out_hbm.at[:, place_ref[0], lon], sems.at[lon]))
    for store in stores:
        store.wait()


IN_VMEM = pl.BlockSpec(memory_space=pltpu.VMEM)
IN_HBM = pl.BlockSpec(memory_space=pltpu.HBM)
ANYWHERE = pl.BlockSpec(memory_space=pl.ANY)
DMA = pltpu.SemaphoreType.DMA


def in_hbm(*arrays):
    return [pltpu.with_memory_space_constraint(x, pltpu.HBM) for x in arrays]


def params(mib):
    return pltpu.CompilerParams(vmem_limit_bytes=mib * MIB)


def scratch(tokens):
    return [
        pltpu.VMEM((tokens, D), F32),
        pltpu.VMEM((tokens, 3 * D), BF),
        pltpu.VMEM((tokens, D), BF),
    ]


def pack(fields):
    return pl.pallas_call(
        pack_kernel,
        in_specs=[ANYWHERE],
        out_specs=IN_VMEM,
        out_shape=pltpu.VMEM((1024, D), BF),
        scratch_shapes=[pltpu.VMEM((64, 4, LEV, D), F32), DMA((8,))],
        compiler_params=params(12),
        name="pack",
    )(*in_hbm(fields))


def longitude(x, gains, qkv_w, out_w, bias):
    return pl.pallas_call(
        longitude_kernel,
        in_specs=[IN_VMEM] * 2 + [ANYWHERE] + [IN_VMEM] * 2,
        out_specs=IN_VMEM,
        out_shape=pltpu.VMEM((1024, D), BF),
        scratch_shapes=[
            pltpu.VMEM((D, 3 * D), BF),
            pltpu.VMEM((1024, D), BF),
            *scratch(1024),
            DMA((3,)),
        ],
        compiler_params=params(24),
        name="longitude",
    )(x, gains, *in_hbm(qkv_w), out_w, bias)


def latitude(member, lat, x, gains, qkv_w, out_w, bias, *late):
    sent = [6] if member else [2, 2]
    return pl.pallas_call(
        lambda *refs: latitude_kernel(member, *refs),
        in_specs=[pl.BlockSpec(memory_space=pltpu.SMEM)] + [IN_VMEM] * (5 + member),
        out_specs=[IN_VMEM] * (1 + len(sent)),
        out_shape=[pltpu.VMEM((LEV, 64, D), F32)] + [pltpu.VMEM((n, 64, D), BF) for n in sent],
        scratch_shapes=scratch(512),
        compiler_params=params(16),
        name="latitude",
    )(lat, x, gains, qkv_w, out_w, bias, *late)


def column(place, pieces, gains, qkv_w, out_w, bias, mlp_in, mlp_out, out=None):
    in_specs = [pl.BlockSpec(memory_space=pltpu.SMEM)] + [IN_VMEM] * 8
    operands = [place, *pieces, gains, qkv_w, out_w, bias, mlp_in, mlp_out]
    aliases = {}
    if out is not None:
        in_specs.append(ANYWHERE)
        operands.append(out)
        aliases = {len(operands) - 1: 0}
    return pl.pallas_call(
        column_kernel,
        in_specs=in_specs,
        out_specs=IN_HBM,
        out_shape=pltpu.HBM((64, 2, 2, LEV, D), F32),
        scratch_shapes=[*scratch(512), pltpu.VMEM((2, 64, LEV, D), F32), DMA((2,))],
        input_output_aliases=aliases,
        compiler_params=params(20),
        name="column",
    )(*operands)


def per_device(
    fields,
    norm_gains,
    qkv_weight,
    out_weight,
    longitude_bias,
    latitude_bias,
    level_bias,
    mlp_in,
    mlp_out,
):
    axes = ("lat", "lon")
    spot = lax.axis_index("lat").astype(jnp.int32).reshape(1)
    fields, spot, other_spot = lax.optimization_barrier((fields, spot, 1 - spot))
    def exchange(x):
        return lax.all_to_all(
            x.reshape(128, 8, D), axes, split_axis=0, concat_axis=0, tiled=True
        ).reshape(1024, D)

    def swap(x):
        return lax.ppermute(x, "lat", [(0, 1), (1, 0)])

    circles = exchange(pack(fields))
    meridians = exchange(longitude(circles, norm_gains, qkv_weight, out_weight, longitude_bias))
    weights = (norm_gains, qkv_weight, out_weight)
    own_first, sent, late = latitude(0, spot, meridians, *weights, latitude_bias)
    own_second, sent_second = latitude(1, spot, meridians, *weights, latitude_bias, late)
    other_first, sent_second = lax.optimization_barrier((swap(sent), sent_second))
    rest = (*weights, level_bias.T, mlp_in, mlp_out)
    out = column(spot, (own_first, own_second), *rest)
    out = column(other_spot, (other_first, swap(sent_second)), *rest, out=out)
    return out.reshape(64, 4, LEV, D)


def solution(mesh):
    in_specs = (P("lat", "lon", None, None), P(), P(), P(), P(), P(), P(), P(), P())
    out_specs = P("lat", "lon", None, None)
    return jax.shard_map(
        per_device, mesh=mesh, in_specs=in_specs, out_specs=out_specs, check_vma=False
    )
```

```python
import math

import jax
import jax.numpy as jnp
from jax import lax
from jax.experimental import pallas as pl
from jax.experimental.pallas import tpu as pltpu
from jax.sharding import PartitionSpec as P

D = 768
HALF = D // 2
HEADS = 12
PAIRS = HEADS // 2
FF = 3072
LEV = 4
EPS = 1e-06
LOG2E = math.log2(math.e)
SCALE = 0.125 * LOG2E
OUTSIDE = -1e30
MIB = 1 << 20
BF = jnp.bfloat16
F32 = jnp.float32


def dot(a, b):
    return lax.dot_general(a, b, (((1,), (0,)), ((), ())), preferred_element_type=F32)


def dot_t(a, b):
    return lax.dot_general(a, b, (((1,), (1,)), ((), ())), preferred_element_type=F32)


def one_hot(rows, cols, target):
    row = lax.broadcasted_iota(jnp.int32, (rows, cols), 0)
    col = lax.broadcasted_iota(jnp.int32, (rows, cols), 1)
    return jnp.where(target(row) == col, 1.0, 0.0).astype(F32).astype(BF)


def normalize(x, gain):
    square = jnp.mean(x * x, axis=-1, keepdims=True)
    return (x * lax.rsqrt(square + EPS) * gain).astype(BF)


def head_masks():
    lane = lax.broadcasted_iota(jnp.int32, (1, 128), 1)
    even = jnp.where(lane < 64, 1.0, 0.0)
    return even.astype(BF), (1.0 - even).astype(BF)


def toeplitz(row, count, shift=0):
    wide = jnp.broadcast_to(row, (count, 256))
    return pltpu.roll(wide, shift, 1, stride=1, stride_axis=0)


def attend_pair(q, k, v, bias):
    even, odd = head_masks()
    rows, count = q.shape[0], k.shape[0]
    scores = dot_t(jnp.concatenate([q * even, q * odd], axis=0), k) * SCALE + bias
    top = jnp.max(scores, axis=-1, keepdims=True)
    weights = jnp.exp2(scores - top).astype(BF)
    ones = [jnp.broadcast_to(mask, (count, 128)) for mask in (even, odd)]
    values = jnp.concatenate(
        [
            jnp.concatenate([v * even, ones[0]], axis=1),
            jnp.concatenate([v * odd, ones[1]], axis=1),
        ],
        axis=0,
    )
    total = dot(jnp.concatenate([weights[:rows], weights[rows:]], axis=1), values)
    return (total[:, :128] / total[:, 128:]).astype(BF)


def fetch(source, target, sem):
    copy = pltpu.make_async_copy(source, target, sem)
    copy.start()
    return copy


def pack_kernel(
    fields_ref,
    lon_ref,
    lat_ref,
    lev_ref,
    out_ref,
    lon_out,
    lat_out,
    lev_out,
    x,
    lon,
    lat,
    lev,
    sems,
    bias_sems,
):
    biases = [
        fetch(source, target, bias_sems.at[n])
        for n, (source, target) in enumerate(((lon_ref, lon), (lat_ref, lat), (lev_ref, lev)))
    ]
    loads = [
        fetch(fields_ref.at[pl.ds(8 * n, 8)], x.at[pl.ds(8 * n, 8)], sems.at[n]) for n in range(8)
    ]
    for bias in biases:
        bias.wait()
    lon_rows = lon[...] * LOG2E
    lat_rows = jnp.concatenate([lat[...], jnp.zeros((HEADS, 1), F32)], axis=1) * LOG2E
    lane = lax.broadcasted_iota(jnp.int32, (1, 256), 1)
    for head in range(HEADS):
        pair, row = head // 2, slice(head, head + 1)
        lev_row = jnp.full((1, 256), OUTSIDE, F32)
        for step in range(1 - LEV, LEV):
            value = lev[step + LEV - 1 : step + LEV, row] * LOG2E
            lev_row = jnp.where(lane == 32 * step % 256, value, lev_row)
        rows = 256 * (head % 2)
        lon_out[pair, rows : rows + 256] = toeplitz(lon_rows[row], 256)
        rows = 128 * (head % 2)
        lat_out[pair, rows : rows + 128] = toeplitz(lat_rows[row], 128, 129)[:, :128]
        lev_out[pair, rows : rows + 128] = toeplitz(lev_row, 128)[:, :128]
    move = one_hot(128, 128, lambda r: r // 16 * 16 + r % 4 * 4 + r // 4 % 4)
    for n in range(8):
        loads[n].wait()
        rows = slice(128 * n, 128 * n + 128)
        out_ref[rows] = dot(move, x[8 * n : 8 * n + 8].reshape(128, D).astype(BF)).astype(BF)


def longitude_kernel(
    x_ref, gains_ref, qkv_w_hbm, out_w, bias_ref, out_ref, qkv_w, x, state, qkv, attended, sems
):
    parts = [pl.ds(D * n, D) for n in range(3)]
    loads = [
        fetch(qkv_w_hbm.at[0, :, part], qkv_w.at[:, part], sems.at[n])
        for n, part in enumerate(parts)
    ]
    move = one_hot(128, 128, lambda t: t % 64 // 4 * 8 + t // 64 * 4 + t % 4)
    for block in range(8):
        moved = dot(move, x_ref[128 * block : 128 * block + 128])
        for level in range(2):
            start = 512 * (block // 4) + 256 * level + 64 * (block % 4)
            state[start : start + 64] = moved[64 * level : 64 * level + 64]
    normed = normalize(state[...], gains_ref[0:1])
    for load, part in zip(loads, parts):
        load.wait()
        qkv[:, part] = dot(normed, qkv_w[:, part]).astype(BF)
    attend_blocks(qkv, attended, bias_ref, [[slice(256 * n, 256 * n + 256)] for n in range(4)])
    x[...] = (state[...] + dot(attended[...], out_w[0])).astype(BF)
    move = one_hot(
        128,
        128,
        lambda r: r // 2 % 4 * 32 + r // 8 % 8 * 4 + r // 64 * 2 + r % 2,
    )
    for block in range(8):
        tokens = jnp.concatenate(
            [x[256 * n + 32 * block : 256 * n + 32 * block + 32] for n in range(4)], axis=0
        )
        moved = dot(move, tokens).astype(BF)
        for lat in range(2):
            start = 512 * lat + 64 * block
            out_ref[start : start + 64] = moved[64 * lat : 64 * lat + 64]


def attend_blocks(qkv, attended, tables, blocks):
    for pair in range(PAIRS):
        cols = [slice(m * D + 128 * pair, m * D + 128 * pair + 128) for m in range(3)]
        table = tables[pair]
        for pieces in blocks:
            q, k, v = (
                jnp.concatenate([qkv[piece, col] for piece in pieces], axis=0) for col in cols
            )
            result = attend_pair(q, k, v, table)
            at = 0
            for piece in pieces:
                size = piece.stop - piece.start
                attended[piece, cols[0]] = result[at : at + size]
                at += size


def latitude_kernel(member, lat_ref, x_ref, gains_ref, qkv_w, out_w, bias_ref, *refs):
    own_ref, *others, state, qkv, attended = refs[member:]
    move = one_hot(
        64,
        128,
        lambda t: t % 8 * 16 + t // 32 * 8 + t // 8 % 2 * 4 + t // 16 % 2 * 2 + member,
    )
    for block in range(8):
        moved = dot(move, x_ref[128 * block : 128 * block + 128])
        for group in range(8):
            start = 64 * group + 8 * block
            state[start : start + 8] = moved[8 * group : 8 * group + 8]
    qkv[...] = dot(normalize(state[...], gains_ref[1:2]), qkv_w[1]).astype(BF)
    attend_blocks(qkv, attended, bias_ref, [[slice(128 * n, 128 * n + 128)] for n in range(4)])
    state[...] = state[...] + dot(attended[...], out_w[1])
    lat = lat_ref[0]
    if member:
        others[0][0:2] = refs[0][...]
        targets = [others[0].at[2 + lev] for lev in range(LEV)]
    else:
        targets = [others[lev // 2].at[lev % 2] for lev in range(LEV)]
    for lev in range(LEV):
        start = pl.multiple_of(128 * lev + 64 * lat, 64)
        own_ref[lev] = state[pl.ds(start, 64)]
        start = pl.multiple_of(128 * lev + 64 * (1 - lat), 64)
        targets[lev][...] = state[pl.ds(start, 64)].astype(BF)


def column_kernel(place_ref, *refs):
    pieces, (gains_ref, qkv_w, out_w, bias_ref, in_w, mlp_w) = refs[:2], refs[2:8]
    out_hbm, state, qkv, attended, result, sems = refs[-6:]
    at = 0
    for piece in pieces:
        size = 64 * piece.shape[0]
        state[at : at + size] = piece[...].reshape(size, D).astype(F32)
        at += size
    qkv[...] = dot(normalize(state[...], gains_ref[2:3]), qkv_w[2]).astype(BF)
    blocks = []
    for lon in range(2):
        for part in range(2):
            starts = [256 * lon + 64 * lev + 32 * part for lev in range(LEV)]
            blocks.append([slice(s, s + 32) for s in starts])
    attend_blocks(qkv, attended, bias_ref, blocks)
    state[...] = state[...] + dot(attended[...], out_w[2])
    normed = normalize(state[...], gains_ref[3:4])
    total = state[...]
    for n in range(4):
        cols = slice(FF // 4 * n, FF // 4 * (n + 1))
        u = dot(normed, in_w[:, cols])
        bend = u * (math.sqrt(2 / math.pi) + (math.sqrt(2 / math.pi) * 0.044715) * (u * u))
        hidden = (0.5 * u * (1.0 + jnp.tanh(bend))).astype(BF)
        if n < 3:
            total = total + dot(hidden, mlp_w[cols])
    stores = []
    for lon in range(2):
        rows = slice(256 * lon, 256 * lon + 256)
        final = total[rows] + dot(hidden[rows], mlp_w[cols])
        for lev in range(LEV):
            result[lon, :, lev, :] = final[64 * lev : 64 * lev + 64]
        stores.append(fetch(result.at[lon], out_hbm.at[:, place_ref[0], lon], sems.at[lon]))
    for store in stores:
        store.wait()


IN_VMEM = pl.BlockSpec(memory_space=pltpu.VMEM)
IN_HBM = pl.BlockSpec(memory_space=pltpu.HBM)
ANYWHERE = pl.BlockSpec(memory_space=pl.ANY)
DMA = pltpu.SemaphoreType.DMA


def in_hbm(*arrays):
    return [pltpu.with_memory_space_constraint(x, pltpu.HBM) for x in arrays]


def params(mib):
    return pltpu.CompilerParams(vmem_limit_bytes=mib * MIB)


def scratch(tokens):
    return [
        pltpu.VMEM((tokens, D), F32),
        pltpu.VMEM((tokens, 3 * D), BF),
        pltpu.VMEM((tokens, D), BF),
    ]


def pack(fields, lon_bias, lat_bias, lev_bias):
    return pl.pallas_call(
        pack_kernel,
        in_specs=[ANYWHERE] * 4,
        out_specs=[IN_VMEM] * 4,
        out_shape=[
            pltpu.VMEM((1024, D), BF),
            pltpu.VMEM((PAIRS, 512, 256), F32),
            pltpu.VMEM((PAIRS, 256, 128), F32),
            pltpu.VMEM((PAIRS, 256, 128), F32),
        ],
        scratch_shapes=[
            pltpu.VMEM((64, 4, LEV, D), F32),
            pltpu.VMEM((HEADS, 256), F32),
            pltpu.VMEM((HEADS, 255), F32),
            pltpu.VMEM((7, HEADS), F32),
            DMA((8,)),
            DMA((3,)),
        ],
        compiler_params=params(12),
        name="pack",
    )(*in_hbm(fields, lon_bias, lat_bias, lev_bias.T))


def longitude(x, gains, qkv_w, out_w, bias):
    return pl.pallas_call(
        longitude_kernel,
        in_specs=[IN_VMEM] * 2 + [ANYWHERE] + [IN_VMEM] * 2,
        out_specs=IN_VMEM,
        out_shape=pltpu.VMEM((1024, D), BF),
        scratch_shapes=[
            pltpu.VMEM((D, 3 * D), BF),
            pltpu.VMEM((1024, D), BF),
            *scratch(1024),
            DMA((3,)),
        ],
        compiler_params=params(24),
        name="longitude",
    )(x, gains, *in_hbm(qkv_w), out_w, bias)


def latitude(member, lat, x, gains, qkv_w, out_w, bias, *late):
    sent = [6] if member else [2, 2]
    return pl.pallas_call(
        lambda *refs: latitude_kernel(member, *refs),
        in_specs=[pl.BlockSpec(memory_space=pltpu.SMEM)] + [IN_VMEM] * (5 + member),
        out_specs=[IN_VMEM] * (1 + len(sent)),
        out_shape=[pltpu.VMEM((LEV, 64, D), F32)] + [pltpu.VMEM((n, 64, D), BF) for n in sent],
        scratch_shapes=scratch(512),
        compiler_params=params(16),
        name="latitude",
    )(lat, x, gains, qkv_w, out_w, bias, *late)


def column(place, pieces, gains, qkv_w, out_w, bias, mlp_in, mlp_out, out=None):
    in_specs = [pl.BlockSpec(memory_space=pltpu.SMEM)] + [IN_VMEM] * 8
    operands = [place, *pieces, gains, qkv_w, out_w, bias, mlp_in, mlp_out]
    aliases = {}
    if out is not None:
        in_specs.append(ANYWHERE)
        operands.append(out)
        aliases = {len(operands) - 1: 0}
    return pl.pallas_call(
        column_kernel,
        in_specs=in_specs,
        out_specs=IN_HBM,
        out_shape=pltpu.HBM((64, 2, 2, LEV, D), F32),
        scratch_shapes=[*scratch(512), pltpu.VMEM((2, 64, LEV, D), F32), DMA((2,))],
        input_output_aliases=aliases,
        compiler_params=params(20),
        name="column",
    )(*operands)


def per_device(
    fields,
    norm_gains,
    qkv_weight,
    out_weight,
    longitude_bias,
    latitude_bias,
    level_bias,
    mlp_in,
    mlp_out,
):
    axes = ("lat", "lon")
    spot = lax.axis_index("lat").astype(jnp.int32).reshape(1)
    fields, spot, other_spot = lax.optimization_barrier((fields, spot, 1 - spot))
    def exchange(x):
        return lax.all_to_all(
            x.reshape(128, 8, D), axes, split_axis=0, concat_axis=0, tiled=True
        ).reshape(1024, D)

    def swap(x):
        return lax.ppermute(x, "lat", [(0, 1), (1, 0)])

    packed, lon_table, lat_table, lev_table = pack(
        fields, longitude_bias, latitude_bias, level_bias
    )
    circles = exchange(packed)
    weights = (norm_gains, qkv_weight, out_weight)
    meridians = exchange(longitude(circles, *weights, lon_table))
    own_first, sent, late = latitude(0, spot, meridians, *weights, lat_table)
    own_second, sent_second = latitude(1, spot, meridians, *weights, lat_table, late)
    other_first, sent_second = lax.optimization_barrier((swap(sent), sent_second))
    rest = (*weights, lev_table, mlp_in, mlp_out)
    out = column(spot, (own_first, own_second), *rest)
    out = column(other_spot, (other_first, swap(sent_second)), *rest, out=out)
    return out.reshape(64, 4, LEV, D)


def solution(mesh):
    in_specs = (P("lat", "lon", None, None), P(), P(), P(), P(), P(), P(), P(), P())
    out_specs = P("lat", "lon", None, None)
    return jax.shard_map(
        per_device, mesh=mesh, in_specs=in_specs, out_specs=out_specs, check_vma=False
    )
```

```python
import math

import jax
import jax.numpy as jnp
from jax import lax
from jax.experimental import pallas as pl
from jax.experimental.pallas import tpu as pltpu
from jax.sharding import PartitionSpec as P

D = 768
HALF = D // 2
HEADS = 12
PAIRS = HEADS // 2
FF = 3072
LEV = 4
EPS = 1e-06
LOG2E = math.log2(math.e)
SCALE = 0.125 * LOG2E
OUTSIDE = -1e30
MIB = 1 << 20
BF = jnp.bfloat16
F32 = jnp.float32


def dot(a, b):
    return lax.dot_general(a, b, (((1,), (0,)), ((), ())), preferred_element_type=F32)


def dot_t(a, b):
    return lax.dot_general(a, b, (((1,), (1,)), ((), ())), preferred_element_type=F32)


def one_hot(rows, cols, target):
    row = lax.broadcasted_iota(jnp.int32, (rows, cols), 0)
    col = lax.broadcasted_iota(jnp.int32, (rows, cols), 1)
    return jnp.where(target(row) == col, 1.0, 0.0).astype(F32).astype(BF)


def normalize(x, gain):
    square = jnp.mean(x * x, axis=-1, keepdims=True)
    return (x * lax.rsqrt(square + EPS) * gain).astype(BF)


def head_masks():
    lane = lax.broadcasted_iota(jnp.int32, (1, 128), 1)
    even = jnp.where(lane < 64, 1.0, 0.0)
    return even.astype(BF), (1.0 - even).astype(BF)


def toeplitz(row, count, shift=0):
    wide = jnp.broadcast_to(row, (count, 256))
    return pltpu.roll(wide, shift, 1, stride=1, stride_axis=0)


def pair_scores(q, k, table):
    even, odd = head_masks()
    return dot_t(jnp.concatenate([q * even, q * odd], axis=0), k) * SCALE + table


def pair_weights(scores):
    top = jnp.max(scores, axis=-1, keepdims=True)
    return jnp.exp2(scores - top).astype(BF)


def pair_values(weights, v):
    even, odd = head_masks()
    rows, count = weights.shape[0] // 2, v.shape[0]
    ones = [jnp.broadcast_to(mask, (count, 128)) for mask in (even, odd)]
    values = jnp.concatenate(
        [
            jnp.concatenate([v * even, ones[0]], axis=1),
            jnp.concatenate([v * odd, ones[1]], axis=1),
        ],
        axis=0,
    )
    total = dot(jnp.concatenate([weights[:rows], weights[rows:]], axis=1), values)
    return (total[:, :128] / total[:, 128:]).astype(BF)


def fetch(source, target, sem):
    copy = pltpu.make_async_copy(source, target, sem)
    copy.start()
    return copy


def pack_kernel(
    fields_ref,
    lon_ref,
    lat_ref,
    lev_ref,
    out_ref,
    lon_out,
    lat_out,
    lev_out,
    x,
    lon,
    lat,
    lev,
    sems,
    bias_sems,
):
    biases = [
        fetch(source, target, bias_sems.at[n])
        for n, (source, target) in enumerate(((lon_ref, lon), (lat_ref, lat), (lev_ref, lev)))
    ]
    loads = [
        fetch(fields_ref.at[pl.ds(8 * n, 8)], x.at[pl.ds(8 * n, 8)], sems.at[n]) for n in range(8)
    ]
    for bias in biases:
        bias.wait()
    lon_rows = lon[...] * LOG2E
    lat_rows = jnp.concatenate([lat[...], jnp.zeros((HEADS, 1), F32)], axis=1) * LOG2E
    lane = lax.broadcasted_iota(jnp.int32, (1, 256), 1)
    for head in range(HEADS):
        pair, row = head // 2, slice(head, head + 1)
        lev_row = jnp.full((1, 256), OUTSIDE, F32)
        for step in range(1 - LEV, LEV):
            value = lev[step + LEV - 1 : step + LEV, row] * LOG2E
            lev_row = jnp.where(lane == 32 * step % 256, value, lev_row)
        rows = 256 * (head % 2)
        lon_out[pair, rows : rows + 256] = toeplitz(lon_rows[row], 256)
        rows = 128 * (head % 2)
        lat_out[pair, rows : rows + 128] = toeplitz(lat_rows[row], 128, 129)[:, :128]
        lev_out[pair, rows : rows + 128] = toeplitz(lev_row, 128)[:, :128]
    move = one_hot(128, 128, lambda r: r // 16 * 16 + r % 4 * 4 + r // 4 % 4)
    for n in range(8):
        loads[n].wait()
        rows = slice(128 * n, 128 * n + 128)
        out_ref[rows] = dot(move, x[8 * n : 8 * n + 8].reshape(128, D).astype(BF)).astype(BF)


def longitude_kernel(
    x_ref, gains_ref, qkv_w_hbm, out_w, bias_ref, out_ref, qkv_w, x, state, qkv, attended, sems
):
    parts = [pl.ds(D * n, D) for n in range(3)]
    loads = [
        fetch(qkv_w_hbm.at[0, :, part], qkv_w.at[:, part], sems.at[n])
        for n, part in enumerate(parts)
    ]
    move = one_hot(128, 128, lambda t: t % 64 // 4 * 8 + t // 64 * 4 + t % 4)
    for block in range(8):
        moved = dot(move, x_ref[128 * block : 128 * block + 128])
        for level in range(2):
            start = 512 * (block // 4) + 256 * level + 64 * (block % 4)
            state[start : start + 64] = moved[64 * level : 64 * level + 64]
    normed = normalize(state[...], gains_ref[0:1])
    for load, part in zip(loads, parts):
        load.wait()
        qkv[:, part] = dot(normed, qkv_w[:, part]).astype(BF)
    attend_blocks(qkv, attended, bias_ref, [[slice(256 * n, 256 * n + 256)] for n in range(4)])
    x[...] = (state[...] + dot(attended[...], out_w[0])).astype(BF)
    move = one_hot(
        128,
        128,
        lambda r: r // 2 % 4 * 32 + r // 8 % 8 * 4 + r // 64 * 2 + r % 2,
    )
    for block in range(8):
        tokens = jnp.concatenate(
            [x[256 * n + 32 * block : 256 * n + 32 * block + 32] for n in range(4)], axis=0
        )
        moved = dot(move, tokens).astype(BF)
        for lat in range(2):
            start = 512 * lat + 64 * block
            out_ref[start : start + 64] = moved[64 * lat : 64 * lat + 64]


def attend_blocks(qkv, attended, tables, blocks, lag=0):
    tasks = [(pair, pieces) for pair in range(PAIRS) for pieces in blocks]

    def read(pair, pieces, member):
        cols = slice(member * D + 128 * pair, member * D + 128 * pair + 128)
        return jnp.concatenate([qkv[piece, cols] for piece in pieces], axis=0)

    def write(pair, pieces, result):
        at = 0
        for piece in pieces:
            size = piece.stop - piece.start
            attended[piece, 128 * pair : 128 * pair + 128] = result[at : at + size]
            at += size

    scores, weights = {}, {}
    for step in range(len(tasks) + lag):
        if step < len(tasks):
            pair, pieces = tasks[step]
            scores[step] = pair_scores(
                read(pair, pieces, 0), read(pair, pieces, 1), tables[pair]
            )
        soft, last = step - lag // 2, step - lag
        if 0 <= soft < len(tasks):
            weights[soft] = pair_weights(scores.pop(soft))
        if last >= 0:
            pair, pieces = tasks[last]
            write(pair, pieces, pair_values(weights.pop(last), read(pair, pieces, 2)))


def latitude_kernel(member, lat_ref, x_ref, gains_ref, qkv_w, out_w, bias_ref, *refs):
    own_ref, *others, state, qkv, attended = refs[member:]
    move = one_hot(
        64,
        128,
        lambda t: t % 8 * 16 + t // 32 * 8 + t // 8 % 2 * 4 + t // 16 % 2 * 2 + member,
    )
    for block in range(8):
        moved = dot(move, x_ref[128 * block : 128 * block + 128])
        for group in range(8):
            start = 64 * group + 8 * block
            state[start : start + 8] = moved[8 * group : 8 * group + 8]
    qkv[...] = dot(normalize(state[...], gains_ref[1:2]), qkv_w[1]).astype(BF)
    attend_blocks(qkv, attended, bias_ref, [[slice(128 * n, 128 * n + 128)] for n in range(4)], 2)
    state[...] = state[...] + dot(attended[...], out_w[1])
    lat = lat_ref[0]
    if member:
        others[0][0:2] = refs[0][...]
        targets = [others[0].at[2 + lev] for lev in range(LEV)]
    else:
        targets = [others[lev // 2].at[lev % 2] for lev in range(LEV)]
    for lev in range(LEV):
        start = pl.multiple_of(128 * lev + 64 * lat, 64)
        own_ref[lev] = state[pl.ds(start, 64)]
        start = pl.multiple_of(128 * lev + 64 * (1 - lat), 64)
        targets[lev][...] = state[pl.ds(start, 64)].astype(BF)


def column_kernel(place_ref, *refs):
    pieces, (gains_ref, qkv_w, out_w, bias_ref, in_w, mlp_w) = refs[:2], refs[2:8]
    out_hbm, state, qkv, attended, result, sems = refs[-6:]
    at = 0
    for piece in pieces:
        size = 64 * piece.shape[0]
        state[at : at + size] = piece[...].reshape(size, D).astype(F32)
        at += size
    qkv[...] = dot(normalize(state[...], gains_ref[2:3]), qkv_w[2]).astype(BF)
    blocks = []
    for lon in range(2):
        for part in range(2):
            starts = [256 * lon + 64 * lev + 32 * part for lev in range(LEV)]
            blocks.append([slice(s, s + 32) for s in starts])
    attend_blocks(qkv, attended, bias_ref, blocks, 2)
    state[...] = state[...] + dot(attended[...], out_w[2])
    normed = normalize(state[...], gains_ref[3:4])
    total = state[...]
    for n in range(4):
        cols = slice(FF // 4 * n, FF // 4 * (n + 1))
        u = dot(normed, in_w[:, cols])
        bend = u * (math.sqrt(2 / math.pi) + (math.sqrt(2 / math.pi) * 0.044715) * (u * u))
        hidden = (0.5 * u * (1.0 + jnp.tanh(bend))).astype(BF)
        if n < 3:
            total = total + dot(hidden, mlp_w[cols])
    stores = []
    for lon in range(2):
        rows = slice(256 * lon, 256 * lon + 256)
        final = total[rows] + dot(hidden[rows], mlp_w[cols])
        for lev in range(LEV):
            result[lon, :, lev, :] = final[64 * lev : 64 * lev + 64]
        stores.append(fetch(result.at[lon], out_hbm.at[:, place_ref[0], lon], sems.at[lon]))
    for store in stores:
        store.wait()


IN_VMEM = pl.BlockSpec(memory_space=pltpu.VMEM)
IN_HBM = pl.BlockSpec(memory_space=pltpu.HBM)
ANYWHERE = pl.BlockSpec(memory_space=pl.ANY)
DMA = pltpu.SemaphoreType.DMA


def in_hbm(*arrays):
    return [pltpu.with_memory_space_constraint(x, pltpu.HBM) for x in arrays]


def params(mib):
    return pltpu.CompilerParams(vmem_limit_bytes=mib * MIB)


def scratch(tokens):
    return [
        pltpu.VMEM((tokens, D), F32),
        pltpu.VMEM((tokens, 3 * D), BF),
        pltpu.VMEM((tokens, D), BF),
    ]


def pack(fields, lon_bias, lat_bias, lev_bias):
    return pl.pallas_call(
        pack_kernel,
        in_specs=[ANYWHERE] * 4,
        out_specs=[IN_VMEM] * 4,
        out_shape=[
            pltpu.VMEM((1024, D), BF),
            pltpu.VMEM((PAIRS, 512, 256), F32),
            pltpu.VMEM((PAIRS, 256, 128), F32),
            pltpu.VMEM((PAIRS, 256, 128), F32),
        ],
        scratch_shapes=[
            pltpu.VMEM((64, 4, LEV, D), F32),
            pltpu.VMEM((HEADS, 256), F32),
            pltpu.VMEM((HEADS, 255), F32),
            pltpu.VMEM((7, HEADS), F32),
            DMA((8,)),
            DMA((3,)),
        ],
        compiler_params=params(12),
        name="pack",
    )(*in_hbm(fields, lon_bias, lat_bias, lev_bias.T))


def longitude(x, gains, qkv_w, out_w, bias):
    return pl.pallas_call(
        longitude_kernel,
        in_specs=[IN_VMEM] * 2 + [ANYWHERE] + [IN_VMEM] * 2,
        out_specs=IN_VMEM,
        out_shape=pltpu.VMEM((1024, D), BF),
        scratch_shapes=[
            pltpu.VMEM((D, 3 * D), BF),
            pltpu.VMEM((1024, D), BF),
            *scratch(1024),
            DMA((3,)),
        ],
        compiler_params=params(24),
        name="longitude",
    )(x, gains, *in_hbm(qkv_w), out_w, bias)


def latitude(member, lat, x, gains, qkv_w, out_w, bias, *late):
    sent = [6] if member else [2, 2]
    return pl.pallas_call(
        lambda *refs: latitude_kernel(member, *refs),
        in_specs=[pl.BlockSpec(memory_space=pltpu.SMEM)] + [IN_VMEM] * (5 + member),
        out_specs=[IN_VMEM] * (1 + len(sent)),
        out_shape=[pltpu.VMEM((LEV, 64, D), F32)] + [pltpu.VMEM((n, 64, D), BF) for n in sent],
        scratch_shapes=scratch(512),
        compiler_params=params(16),
        name="latitude",
    )(lat, x, gains, qkv_w, out_w, bias, *late)


def column(place, pieces, gains, qkv_w, out_w, bias, mlp_in, mlp_out, out=None):
    in_specs = [pl.BlockSpec(memory_space=pltpu.SMEM)] + [IN_VMEM] * 8
    operands = [place, *pieces, gains, qkv_w, out_w, bias, mlp_in, mlp_out]
    aliases = {}
    if out is not None:
        in_specs.append(ANYWHERE)
        operands.append(out)
        aliases = {len(operands) - 1: 0}
    return pl.pallas_call(
        column_kernel,
        in_specs=in_specs,
        out_specs=IN_HBM,
        out_shape=pltpu.HBM((64, 2, 2, LEV, D), F32),
        scratch_shapes=[*scratch(512), pltpu.VMEM((2, 64, LEV, D), F32), DMA((2,))],
        input_output_aliases=aliases,
        compiler_params=params(20),
        name="column",
    )(*operands)


def per_device(
    fields,
    norm_gains,
    qkv_weight,
    out_weight,
    longitude_bias,
    latitude_bias,
    level_bias,
    mlp_in,
    mlp_out,
):
    axes = ("lat", "lon")
    spot = lax.axis_index("lat").astype(jnp.int32).reshape(1)
    fields, spot, other_spot = lax.optimization_barrier((fields, spot, 1 - spot))
    def exchange(x):
        return lax.all_to_all(
            x.reshape(128, 8, D), axes, split_axis=0, concat_axis=0, tiled=True
        ).reshape(1024, D)

    def swap(x):
        return lax.ppermute(x, "lat", [(0, 1), (1, 0)])

    packed, lon_table, lat_table, lev_table = pack(
        fields, longitude_bias, latitude_bias, level_bias
    )
    circles = exchange(packed)
    weights = (norm_gains, qkv_weight, out_weight)
    meridians = exchange(longitude(circles, *weights, lon_table))
    own_first, sent, late = latitude(0, spot, meridians, *weights, lat_table)
    own_second, sent_second = latitude(1, spot, meridians, *weights, lat_table, late)
    other_first, sent_second = lax.optimization_barrier((swap(sent), sent_second))
    rest = (*weights, lev_table, mlp_in, mlp_out)
    out = column(spot, (own_first, own_second), *rest)
    out = column(other_spot, (other_first, swap(sent_second)), *rest, out=out)
    return out.reshape(64, 4, LEV, D)


def solution(mesh):
    in_specs = (P("lat", "lon", None, None), P(), P(), P(), P(), P(), P(), P(), P())
    out_specs = P("lat", "lon", None, None)
    return jax.shard_map(
        per_device, mesh=mesh, in_specs=in_specs, out_specs=out_specs, check_vma=False
    )
```

```python
import math

import jax
import jax.numpy as jnp
from jax import lax
from jax.experimental import pallas as pl
from jax.experimental.pallas import tpu as pltpu
from jax.sharding import PartitionSpec as P

D = 768
HALF = D // 2
HEADS = 12
PAIRS = HEADS // 2
FF = 3072
LEV = 4
EPS = 1e-06
LOG2E = math.log2(math.e)
SCALE = 0.125 * LOG2E
OUTSIDE = -1e30
MIB = 1 << 20
BF = jnp.bfloat16
F32 = jnp.float32


def dot(a, b):
    return lax.dot_general(a, b, (((1,), (0,)), ((), ())), preferred_element_type=F32)


def dot_t(a, b):
    return lax.dot_general(a, b, (((1,), (1,)), ((), ())), preferred_element_type=F32)


def one_hot(rows, cols, target):
    row = lax.broadcasted_iota(jnp.int32, (rows, cols), 0)
    col = lax.broadcasted_iota(jnp.int32, (rows, cols), 1)
    return jnp.where(target(row) == col, 1.0, 0.0).astype(F32).astype(BF)


def normalize(x, gain):
    square = jnp.mean(x * x, axis=-1, keepdims=True)
    return (x * lax.rsqrt(square + EPS) * gain).astype(BF)


def head_masks():
    lane = lax.broadcasted_iota(jnp.int32, (1, 128), 1)
    even = jnp.where(lane < 64, 1.0, 0.0)
    return even.astype(BF), (1.0 - even).astype(BF)


def toeplitz(row, count, shift=0):
    wide = jnp.broadcast_to(row, (count, 256))
    return pltpu.roll(wide, shift, 1, stride=1, stride_axis=0)


def pair_scores(q, k, table):
    even, odd = head_masks()
    return dot_t(jnp.concatenate([q * even, q * odd], axis=0), k) * SCALE + table


def pair_weights(scores):
    top = jnp.max(scores, axis=-1, keepdims=True)
    return jnp.exp2(scores - top).astype(BF)


def pair_values(weights, v):
    even, odd = head_masks()
    rows, count = weights.shape[0] // 2, v.shape[0]
    ones = [jnp.broadcast_to(mask, (count, 128)) for mask in (even, odd)]
    values = jnp.concatenate(
        [
            jnp.concatenate([v * even, ones[0]], axis=1),
            jnp.concatenate([v * odd, ones[1]], axis=1),
        ],
        axis=0,
    )
    total = dot(jnp.concatenate([weights[:rows], weights[rows:]], axis=1), values)
    return (total[:, :128] / total[:, 128:]).astype(BF)


def fetch(source, target, sem):
    copy = pltpu.make_async_copy(source, target, sem)
    copy.start()
    return copy


def pack_kernel(
    fields_ref,
    lon_ref,
    lat_ref,
    lev_ref,
    out_ref,
    lon_out,
    lat_out,
    lev_out,
    x,
    lon,
    lat,
    lev,
    sems,
    bias_sems,
):
    biases = [
        fetch(source, target, bias_sems.at[n])
        for n, (source, target) in enumerate(((lon_ref, lon), (lat_ref, lat), (lev_ref, lev)))
    ]
    loads = [
        fetch(fields_ref.at[pl.ds(8 * n, 8)], x.at[pl.ds(8 * n, 8)], sems.at[n]) for n in range(8)
    ]
    for bias in biases:
        bias.wait()
    lon_rows = lon[...] * LOG2E
    lat_rows = jnp.concatenate([lat[...], jnp.zeros((HEADS, 1), F32)], axis=1) * LOG2E
    lane = lax.broadcasted_iota(jnp.int32, (1, 256), 1)
    for head in range(HEADS):
        pair, row = head // 2, slice(head, head + 1)
        lev_row = jnp.full((1, 256), OUTSIDE, F32)
        for step in range(1 - LEV, LEV):
            value = lev[step + LEV - 1 : step + LEV, row] * LOG2E
            lev_row = jnp.where(lane == 32 * step % 256, value, lev_row)
        rows = 256 * (head % 2)
        lon_out[pair, rows : rows + 256] = toeplitz(lon_rows[row], 256)
        rows = 128 * (head % 2)
        lat_out[pair, rows : rows + 128] = toeplitz(lat_rows[row], 128, 129)[:, :128]
        lev_out[pair, rows : rows + 128] = toeplitz(lev_row, 128)[:, :128]
    move = one_hot(128, 128, lambda r: r // 16 * 16 + r % 4 * 4 + r // 4 % 4)
    for n in range(8):
        loads[n].wait()
        rows = slice(128 * n, 128 * n + 128)
        out_ref[rows] = dot(move, x[8 * n : 8 * n + 8].reshape(128, D).astype(BF)).astype(BF)


def longitude_kernel(
    x_ref, gains_ref, qkv_w_hbm, out_w, bias_ref, out_ref, qkv_w, x, state, qkv, attended, sems
):
    parts = [pl.ds(D * n, D) for n in range(3)]
    loads = [
        fetch(qkv_w_hbm.at[0, :, part], qkv_w.at[:, part], sems.at[n])
        for n, part in enumerate(parts)
    ]
    move = one_hot(128, 128, lambda t: t % 64 // 4 * 8 + t // 64 * 4 + t % 4)
    for block in range(8):
        moved = dot(move, x_ref[128 * block : 128 * block + 128])
        for level in range(2):
            start = 512 * (block // 4) + 256 * level + 64 * (block % 4)
            state[start : start + 64] = moved[64 * level : 64 * level + 64]
    normed = normalize(state[...], gains_ref[0:1])
    for load, part in zip(loads, parts):
        load.wait()
        qkv[:, part] = dot(normed, qkv_w[:, part]).astype(BF)
    attend_blocks(qkv, attended, bias_ref, [[slice(256 * n, 256 * n + 256)] for n in range(4)], 2, 2)
    x[...] = (state[...] + dot(attended[...], out_w[0])).astype(BF)
    move = one_hot(
        128,
        128,
        lambda r: r // 2 % 4 * 32 + r // 8 % 8 * 4 + r // 64 * 2 + r % 2,
    )
    for block in range(8):
        tokens = jnp.concatenate(
            [x[256 * n + 32 * block : 256 * n + 32 * block + 32] for n in range(4)], axis=0
        )
        moved = dot(move, tokens).astype(BF)
        for lat in range(2):
            start = 512 * lat + 64 * block
            out_ref[start : start + 64] = moved[64 * lat : 64 * lat + 64]


def attend_blocks(qkv, attended, tables, blocks, lag, split=1):
    tasks = [
        (pair, pieces, part) for pair in range(PAIRS) for pieces in blocks for part in range(split)
    ]

    def queries(pieces, part):
        sizes = [(piece.stop - piece.start) // split for piece in pieces]
        return [slice(p.start + part * n, p.start + part * n + n) for p, n in zip(pieces, sizes)]

    def read(pair, pieces, member):
        cols = slice(member * D + 128 * pair, member * D + 128 * pair + 128)
        return jnp.concatenate([qkv[piece, cols] for piece in pieces], axis=0)

    def table_of(pair, part):
        if split == 1:
            return tables[pair]
        half = tables.shape[1] // 2
        size = half // split
        starts = [half * e + size * part for e in range(2)]
        return jnp.concatenate([tables[pair, at : at + size] for at in starts], axis=0)

    def write(pair, pieces, result):
        at = 0
        for piece in pieces:
            size = piece.stop - piece.start
            attended[piece, 128 * pair : 128 * pair + 128] = result[at : at + size]
            at += size

    scores, weights = {}, {}
    for step in range(len(tasks) + lag):
        if step < len(tasks):
            pair, pieces, part = tasks[step]
            scores[step] = pair_scores(
                read(pair, queries(pieces, part), 0), read(pair, pieces, 1), table_of(pair, part)
            )
        soft, last = step - lag // 2, step - lag
        if 0 <= soft < len(tasks):
            weights[soft] = pair_weights(scores.pop(soft))
        if last >= 0:
            pair, pieces, part = tasks[last]
            result = pair_values(weights.pop(last), read(pair, pieces, 2))
            write(pair, queries(pieces, part), result)


def latitude_kernel(member, lat_ref, x_ref, gains_ref, qkv_w, out_w, bias_ref, *refs):
    own_ref, *others, state, qkv, attended = refs[member:]
    move = one_hot(
        64,
        128,
        lambda t: t % 8 * 16 + t // 32 * 8 + t // 8 % 2 * 4 + t // 16 % 2 * 2 + member,
    )
    for block in range(8):
        moved = dot(move, x_ref[128 * block : 128 * block + 128])
        for group in range(8):
            start = 64 * group + 8 * block
            state[start : start + 8] = moved[8 * group : 8 * group + 8]
    qkv[...] = dot(normalize(state[...], gains_ref[1:2]), qkv_w[1]).astype(BF)
    attend_blocks(qkv, attended, bias_ref, [[slice(128 * n, 128 * n + 128)] for n in range(4)], 2)
    state[...] = state[...] + dot(attended[...], out_w[1])
    lat = lat_ref[0]
    if member:
        others[0][0:2] = refs[0][...]
        targets = [others[0].at[2 + lev] for lev in range(LEV)]
    else:
        targets = [others[lev // 2].at[lev % 2] for lev in range(LEV)]
    for lev in range(LEV):
        start = pl.multiple_of(128 * lev + 64 * lat, 64)
        own_ref[lev] = state[pl.ds(start, 64)]
        start = pl.multiple_of(128 * lev + 64 * (1 - lat), 64)
        targets[lev][...] = state[pl.ds(start, 64)].astype(BF)


def column_kernel(place_ref, *refs):
    pieces, (gains_ref, qkv_w, out_w, bias_ref, in_w, mlp_w) = refs[:2], refs[2:8]
    out_hbm, state, qkv, attended, result, sems = refs[-6:]
    at = 0
    for piece in pieces:
        size = 64 * piece.shape[0]
        state[at : at + size] = piece[...].reshape(size, D).astype(F32)
        at += size
    qkv[...] = dot(normalize(state[...], gains_ref[2:3]), qkv_w[2]).astype(BF)
    blocks = []
    for lon in range(2):
        for part in range(2):
            starts = [256 * lon + 64 * lev + 32 * part for lev in range(LEV)]
            blocks.append([slice(s, s + 32) for s in starts])
    attend_blocks(qkv, attended, bias_ref, blocks, 2)
    state[...] = state[...] + dot(attended[...], out_w[2])
    normed = normalize(state[...], gains_ref[3:4])
    total = state[...]
    for n in range(4):
        cols = slice(FF // 4 * n, FF // 4 * (n + 1))
        u = dot(normed, in_w[:, cols])
        bend = u * (math.sqrt(2 / math.pi) + (math.sqrt(2 / math.pi) * 0.044715) * (u * u))
        hidden = (0.5 * u * (1.0 + jnp.tanh(bend))).astype(BF)
        if n < 3:
            total = total + dot(hidden, mlp_w[cols])
    stores = []
    for lon in range(2):
        rows = slice(256 * lon, 256 * lon + 256)
        final = total[rows] + dot(hidden[rows], mlp_w[cols])
        for lev in range(LEV):
            result[lon, :, lev, :] = final[64 * lev : 64 * lev + 64]
        stores.append(fetch(result.at[lon], out_hbm.at[:, place_ref[0], lon], sems.at[lon]))
    for store in stores:
        store.wait()


IN_VMEM = pl.BlockSpec(memory_space=pltpu.VMEM)
IN_HBM = pl.BlockSpec(memory_space=pltpu.HBM)
ANYWHERE = pl.BlockSpec(memory_space=pl.ANY)
DMA = pltpu.SemaphoreType.DMA


def in_hbm(*arrays):
    return [pltpu.with_memory_space_constraint(x, pltpu.HBM) for x in arrays]


def params(mib):
    return pltpu.CompilerParams(vmem_limit_bytes=mib * MIB)


def scratch(tokens):
    return [
        pltpu.VMEM((tokens, D), F32),
        pltpu.VMEM((tokens, 3 * D), BF),
        pltpu.VMEM((tokens, D), BF),
    ]


def pack(fields, lon_bias, lat_bias, lev_bias):
    return pl.pallas_call(
        pack_kernel,
        in_specs=[ANYWHERE] * 4,
        out_specs=[IN_VMEM] * 4,
        out_shape=[
            pltpu.VMEM((1024, D), BF),
            pltpu.VMEM((PAIRS, 512, 256), F32),
            pltpu.VMEM((PAIRS, 256, 128), F32),
            pltpu.VMEM((PAIRS, 256, 128), F32),
        ],
        scratch_shapes=[
            pltpu.VMEM((64, 4, LEV, D), F32),
            pltpu.VMEM((HEADS, 256), F32),
            pltpu.VMEM((HEADS, 255), F32),
            pltpu.VMEM((7, HEADS), F32),
            DMA((8,)),
            DMA((3,)),
        ],
        compiler_params=params(12),
        name="pack",
    )(*in_hbm(fields, lon_bias, lat_bias, lev_bias.T))


def longitude(x, gains, qkv_w, out_w, bias):
    return pl.pallas_call(
        longitude_kernel,
        in_specs=[IN_VMEM] * 2 + [ANYWHERE] + [IN_VMEM] * 2,
        out_specs=IN_VMEM,
        out_shape=pltpu.VMEM((1024, D), BF),
        scratch_shapes=[
            pltpu.VMEM((D, 3 * D), BF),
            pltpu.VMEM((1024, D), BF),
            *scratch(1024),
            DMA((3,)),
        ],
        compiler_params=params(24),
        name="longitude",
    )(x, gains, *in_hbm(qkv_w), out_w, bias)


def latitude(member, lat, x, gains, qkv_w, out_w, bias, *late):
    sent = [6] if member else [2, 2]
    return pl.pallas_call(
        lambda *refs: latitude_kernel(member, *refs),
        in_specs=[pl.BlockSpec(memory_space=pltpu.SMEM)] + [IN_VMEM] * (5 + member),
        out_specs=[IN_VMEM] * (1 + len(sent)),
        out_shape=[pltpu.VMEM((LEV, 64, D), F32)] + [pltpu.VMEM((n, 64, D), BF) for n in sent],
        scratch_shapes=scratch(512),
        compiler_params=params(16),
        name="latitude",
    )(lat, x, gains, qkv_w, out_w, bias, *late)


def column(place, pieces, gains, qkv_w, out_w, bias, mlp_in, mlp_out, out=None):
    in_specs = [pl.BlockSpec(memory_space=pltpu.SMEM)] + [IN_VMEM] * 8
    operands = [place, *pieces, gains, qkv_w, out_w, bias, mlp_in, mlp_out]
    aliases = {}
    if out is not None:
        in_specs.append(ANYWHERE)
        operands.append(out)
        aliases = {len(operands) - 1: 0}
    return pl.pallas_call(
        column_kernel,
        in_specs=in_specs,
        out_specs=IN_HBM,
        out_shape=pltpu.HBM((64, 2, 2, LEV, D), F32),
        scratch_shapes=[*scratch(512), pltpu.VMEM((2, 64, LEV, D), F32), DMA((2,))],
        input_output_aliases=aliases,
        compiler_params=params(20),
        name="column",
    )(*operands)


def per_device(
    fields,
    norm_gains,
    qkv_weight,
    out_weight,
    longitude_bias,
    latitude_bias,
    level_bias,
    mlp_in,
    mlp_out,
):
    axes = ("lat", "lon")
    spot = lax.axis_index("lat").astype(jnp.int32).reshape(1)
    fields, spot, other_spot = lax.optimization_barrier((fields, spot, 1 - spot))
    def exchange(x):
        return lax.all_to_all(
            x.reshape(128, 8, D), axes, split_axis=0, concat_axis=0, tiled=True
        ).reshape(1024, D)

    def swap(x):
        return lax.ppermute(x, "lat", [(0, 1), (1, 0)])

    packed, lon_table, lat_table, lev_table = pack(
        fields, longitude_bias, latitude_bias, level_bias
    )
    circles = exchange(packed)
    weights = (norm_gains, qkv_weight, out_weight)
    meridians = exchange(longitude(circles, *weights, lon_table))
    own_first, sent, late = latitude(0, spot, meridians, *weights, lat_table)
    own_second, sent_second = latitude(1, spot, meridians, *weights, lat_table, late)
    other_first, sent_second = lax.optimization_barrier((swap(sent), sent_second))
    rest = (*weights, lev_table, mlp_in, mlp_out)
    out = column(spot, (own_first, own_second), *rest)
    out = column(other_spot, (other_first, swap(sent_second)), *rest, out=out)
    return out.reshape(64, 4, LEV, D)


def solution(mesh):
    in_specs = (P("lat", "lon", None, None), P(), P(), P(), P(), P(), P(), P(), P())
    out_specs = P("lat", "lon", None, None)
    return jax.shard_map(
        per_device, mesh=mesh, in_specs=in_specs, out_specs=out_specs, check_vma=False
    )
```
